32 devices in a mesh: section: 16 (over z, y, x), replica: 2 (over core).
Axes of the slice: x: 2, y: 2, z: 4, core: 2. Of those that a mesh axis runs over, the one named last changes fastest.
Arguments:
- features: bfloat16 [16384, 256], P(('section', 'replica')), may hold values from -6 to 6
- adj_tiles: bfloat16 [4096, 128, 128], P(('section', 'replica')), may hold values from 0.0029907227 to 0.039794922
- tile_index: int32 [4096, 2], P(('section', 'replica')), may hold values from -1 to 7, as said below
- weight: bfloat16 [256, 256], replicated, may hold values from -0.375 to 0.375
- bias_vec: float32 [256], replicated, may hold values from -4 to 4
- grad_out: bfloat16 [16384, 256], P(('section', 'replica'))
Outputs:
- output: bfloat16 [16384, 256], P(('section', 'replica'))
- grad_weight: float32 [256, 256], replicated
- grad_bias: float32 [256], replicated
The draws below stay inside these ranges and needn't reach their ends.
Inputs may be any that keep to these rules, and one draw needn't show every extreme that they name: `tile_index`: entry [k, 0] is a row block within the slab, or -1 for an empty slot; entry [k, 1] is a column block within the column section's slab, 0 in empty slots. Within each group of 16 slots the live slots come first and their (row, column) pairs are distinct; every group has a live slot, and some group is full.
All inputs are finite; a program needn't handle non-finite values.
Results may differ from the reference program's by a relative error of at most 0.0051.
Values may be sent and summed in bfloat16 or wider, within the bound.
No kernel may reach another device: no remote copies, remote signals or barrier semaphores. Data moves between devices by JAX's collectives and lax.ppermute only.
A program may use at most 64 MiB of HBM per device.

```python
import math
import jax
import jax.numpy as jnp
from jax import lax

D = 256
BLOCK = 128
RB = 8
SLOT = 16
TURNS = 8
NODES = 16384
TILES = 4096
N_SECTION = 16
N_REPLICA = 2


def draw_tile_index(key, part):
    group_total = TILES // SLOT
    key_count, key_full, key_perm = jax.random.split(key, 3)
    squares = jax.random.randint(key_count, (group_total,), 0, 64)
    least = max(SLOT // 8, 1)
    counts = least + (SLOT - least) * squares * squares // 4096
    full_group = jax.random.randint(key_full, (), 0, group_total)
    counts = jnp.where(jnp.arange(group_total) == full_group, SLOT, counts)

    def pick_order(sub_key):
        return jax.random.permutation(sub_key, RB * RB)
    orders = jax.vmap(pick_order)(jax.random.split(key_perm, group_total))[:, :SLOT]
    live = jnp.arange(SLOT)[None, :] < counts[:, None]
    row_part = jnp.where(live, orders // RB, -1)
    col_part = jnp.where(live, orders % RB, 0)
    return jnp.stack([row_part, col_part], axis=-1).reshape(TILES, 2).astype(jnp.int32)


def draw_grad_out(key, part):
    key_base = jax.random.fold_in(key, 0)
    ramp = 1.0 + 2.0 * jnp.arange(NODES, dtype=jnp.float32) / max(NODES - 1, 1)
    base = jax.random.normal(key_base, (NODES, D), jnp.float32)
    return (base * ramp[:, None] / math.sqrt(NODES)).astype(jnp.bfloat16)


def level_of(own_key, dims, pieces, low, high):
    level = 1.0
    for axis_at, shards_of in pieces:
        draws = jax.random.uniform(jax.random.fold_in(jax.random.fold_in(own_key, 6), axis_at), (shards_of,), jnp.float32, low / len(pieces), high / len(pieces))
        level = level * jnp.repeat(jnp.exp(draws), dims[axis_at] // shards_of).reshape((-1,) + (1,) * (len(dims) - 1 - axis_at))
    return level


def bell_draw(stream_key, dims, deviation, limit, pieces=(), kind=jnp.bfloat16):
    result = deviation * jax.random.normal(stream_key, dims, jnp.float32)
    if pieces:
        result = result * level_of(stream_key, dims, pieces, -0.22, 0.18)
    return jnp.clip(result, -limit, limit).astype(kind)


def setup_inputs(seed: int = 0) -> dict:
    key_list = jax.random.split(jax.random.key(seed), 7)
    return {
        "features": bell_draw(key_list[0], (NODES, D), 1.0, 6.0, ((0, 32),)),
        "adj_tiles": jnp.clip(jnp.exp(math.log(0.039794922) - 2.58822426 * jax.random.uniform(key_list[1], (TILES, BLOCK, BLOCK), jnp.float32) ** level_of(key_list[1], (TILES, BLOCK, BLOCK), ((0, 32),), -0.2, 0.2)), 0.0029907227, 0.039794922).astype(jnp.bfloat16),
        "tile_index": draw_tile_index(jax.random.fold_in(key_list[6], 71), 0),
        "weight": bell_draw(key_list[3], (D, D), D ** -0.5, 0.375),
        "bias_vec": bell_draw(key_list[4], (D,), 1.0, 4.0, (), jnp.float32),
        "grad_out": draw_grad_out(jax.random.fold_in(key_list[6], 71), 0),
    }


def reference(features, adj_tiles, tile_index, weight, bias_vec, grad_out):
    col_section = jnp.arange(N_REPLICA, dtype=jnp.int32)[:, None] * TURNS + jnp.arange(TURNS, dtype=jnp.int32)[None, :]
    feat_blocks = features.reshape(N_SECTION * RB, BLOCK, D)
    tiles_all = adj_tiles.reshape(N_SECTION, N_REPLICA * TURNS * SLOT, BLOCK, BLOCK)
    index_all = tile_index.reshape(N_SECTION, N_REPLICA, TURNS, SLOT, 2)
    levels = jnp.arange(RB, dtype=jnp.int32)

    def one_section(pair):
        section_tiles, section_index = pair
        global_cols = (col_section[:, :, None] * RB + section_index[..., 1]).reshape(-1).astype(jnp.int32)
        row_pick = section_index[..., 0].reshape(-1).astype(jnp.int32)
        picked = feat_blocks[global_cols].astype(jnp.float32)
        products = jnp.einsum("kab,kbd->kad", section_tiles.astype(jnp.float32), picked, precision=lax.Precision.HIGHEST)
        onehot = (row_pick[:, None] == levels[None, :]).astype(jnp.float32)
        return jnp.einsum("kr,kad->rad", onehot, products, precision=lax.Precision.HIGHEST)

    aggregated = lax.map(one_section, (tiles_all, index_all)).reshape(NODES, D)
    hidden = aggregated.astype(jnp.bfloat16)
    pre_act = jnp.dot(hidden, weight, preferred_element_type=jnp.float32) + bias_vec
    output = jax.nn.silu(pre_act).astype(jnp.bfloat16)
    sigma = jax.nn.sigmoid(pre_act)
    grad_pre = grad_out.astype(jnp.float32) * sigma * (1.0 + pre_act * (1.0 - sigma))
    grad_low = grad_pre.astype(jnp.bfloat16)
    grad_weight = jnp.einsum("nd,ne->de", hidden.astype(jnp.float32), grad_low.astype(jnp.float32), precision=lax.Precision.HIGHEST)
    grad_bias = jnp.sum(grad_pre, axis=0)
    return output, grad_weight, grad_bias
```

```python
import functools

import jax
import jax.numpy as jnp
from jax import lax
from jax.experimental import pallas as pl
from jax.experimental.pallas import tpu as pltpu
from jax.sharding import PartitionSpec as P

BOTH = ("section", "replica")
VMEM = pltpu.VMEM
SMEM = pltpu.SMEM


def spread(x, axis, root):
    mine = lax.axis_index(axis) == root
    return lax.psum(jnp.where(mine, x, jnp.zeros_like(x)), axis)


def add_tiles(summed, received, adj_tiles, row_ids, col_ids, first_slot, count, levels):
    tile_part = lax.dynamic_slice_in_dim(adj_tiles, first_slot, count, 0)
    row_pick = lax.dynamic_slice_in_dim(row_ids, first_slot, count, 0)
    col_pick = lax.dynamic_slice_in_dim(col_ids, first_slot, count, 0)
    picked = received[col_pick]
    products = jnp.einsum("kab,kbd->kad", tile_part, picked, preferred_element_type=jnp.float32)
    onehot = (row_pick[:, None] == levels[None, :]).astype(jnp.float32)
    return summed + jnp.einsum("kr,kad->rad", onehot, products, precision=lax.Precision.HIGHEST)


def general_shards(features, adj_tiles, tile_index, weight, bias_vec, grad_out):
    replicas = lax.axis_size("replica")
    replica_idx = lax.axis_index("replica")
    own_slab = lax.all_gather(features, "replica", axis=0, tiled=True)
    rows_slab, feat_width = own_slab.shape
    block_size = adj_tiles.shape[1]
    row_blocks = rows_slab // block_size
    turn_count = lax.axis_size("section") // replicas
    slot_count = adj_tiles.shape[0] // turn_count
    row_ids = tile_index[:, 0]
    col_ids = tile_index[:, 1]
    levels = jnp.arange(row_blocks, dtype=jnp.int32)

    def turn_step(step_idx, summed):
        received = spread(own_slab, "section", replica_idx * turn_count + step_idx)
        received = received.reshape(row_blocks, block_size, feat_width)
        first_slot = step_idx * slot_count
        return add_tiles(
            summed, received, adj_tiles, row_ids, col_ids, first_slot, slot_count, levels
        )

    start_sum = jnp.zeros((row_blocks, block_size, feat_width), jnp.float32)
    partial_sum = lax.fori_loop(0, turn_count, turn_step, start_sum).reshape(rows_slab, feat_width)
    share = rows_slab // replicas
    whole_sum = lax.psum(partial_sum, "replica")
    local_rows = lax.dynamic_slice_in_dim(whole_sum, replica_idx * share, share, 0)
    hidden = local_rows.astype(jnp.bfloat16)
    pre_act = jnp.dot(hidden, weight, preferred_element_type=jnp.float32) + bias_vec
    output = jax.nn.silu(pre_act).astype(jnp.bfloat16)
    sigma = jax.nn.sigmoid(pre_act)
    grad_pre = grad_out.astype(jnp.float32) * sigma * (1.0 + pre_act * (1.0 - sigma))
    grad_low = grad_pre.astype(jnp.bfloat16)
    weight_term = jnp.einsum("nd,ne->de", hidden, grad_low, preferred_element_type=jnp.float32)
    grad_weight, grad_bias = lax.psum((weight_term, jnp.sum(grad_pre, axis=0)), BOTH)
    return (output, grad_weight, grad_bias)


def send(x, target, name):
    perm = [(2 * p + c, 2 * target(p, c) + c) for p in range(16) for c in range(2)]
    with jax.named_scope(name):
        return lax.ppermute(x, BOTH, perm)


def swap(x, name):
    with jax.named_scope(name):
        return lax.ppermute(x, "replica", [(0, 1), (1, 0)])


def first_hop(x, name):
    return send(x, lambda p, c: p ^ (1 if c == 0 else 2), name)


def second_hop(x, name):
    return send(x, lambda p, c: p ^ (2 if c == 0 else 1), name)


def along_z(x, k, name):
    return send(x, lambda p, c: p ^ (4 * k), name)


def work_list(index_own, index_other, slots, row_blocks):
    chip = lax.axis_index("section")
    core = lax.axis_index("replica")
    half = row_blocks // 2
    count = index_own.shape[0]
    index = jnp.concatenate([index_own, index_other], axis=0)
    tile = jnp.arange(2 * count, dtype=jnp.int32)
    turns = count // slots
    owner = jnp.where(tile < count, core, 1 - core)
    source = owner * turns + (tile % count) // slots
    row, col = index[:, 0], index[:, 1]
    live = (row >= 0) & (col // half == core)
    apart = source ^ chip
    x_apart, y_apart, z_apart = apart & 1, (apart >> 1) & 1, apart >> 2
    near = jnp.where(core == 0, x_apart, y_apart)
    far = jnp.where(core == 0, y_apart, x_apart)
    groups = 8
    group = jnp.where(live, 2 * z_apart + far, groups)
    block = half * near + col % half
    entry = tile | (block << 8) | ((row ^ (half * core)) << 12)
    spare = row_blocks << 12
    sizes = jnp.sum((group[:, None] == jnp.arange(groups)[None, :]).astype(jnp.int32), axis=0)
    padded = (sizes + 1) // 2 * 2
    edge = jnp.arange(groups + 1)
    starts = jnp.sum(jnp.where(edge[None, :groups] < edge[:, None], padded[None, :], 0), axis=1)
    same = (group[:, None] == group[None, :]) & (tile[None, :] < tile[:, None])
    rank = jnp.sum(same.astype(jnp.int32), axis=1)
    base = jnp.sum(jnp.where(group[:, None] == edge[None, :groups], starts[None, :groups], 0), axis=1)
    place = jnp.where(live, base + rank, -1)
    length = 2 * count + 2 * groups
    hit = place[None, :] == jnp.arange(length, dtype=jnp.int32)[:, None]
    entries = spare + jnp.sum(jnp.where(hit, (entry - spare)[None, :], 0), axis=1)
    return entries, starts


def gather_kernel(count, entries, starts, own, other, out, sem):
    total = starts[8]

    def begin(m, carry):
        tile = entries[m] & 255

        @pl.when(tile < count)
        def _():
            pltpu.make_async_copy(own.at[tile], out.at[m], sem).start()

        @pl.when(tile >= count)
        def _():
            pltpu.make_async_copy(other.at[tile - count], out.at[m], sem).start()

        return carry

    def finish(m, carry):
        pltpu.make_async_copy(own.at[0], out.at[0], sem).wait()
        return carry

    lax.fori_loop(0, total, begin, 0)
    lax.fori_loop(0, total, finish, 0)


def gather_tiles(entries, starts, own, other):
    size = own.shape[1]
    return pl.pallas_call(
        functools.partial(gather_kernel, own.shape[0]),
        out_shape=VMEM((entries.shape[0], size, size), own.dtype),
        in_specs=[pl.BlockSpec(memory_space=SMEM)] * 2 + [pl.BlockSpec(memory_space=pl.ANY)] * 2,
        out_specs=pl.BlockSpec(memory_space=VMEM),
        scratch_shapes=[pltpu.SemaphoreType.DMA],
        name="gather_tiles",
        compiler_params=pltpu.CompilerParams(vmem_limit_bytes=1 << 20),
        cost_estimate=pl.CostEstimate(flops=0, bytes_accessed=4 << 20, transcendentals=0),
    )(entries, starts, own, other)


def add_group(entries, lo, hi, tiles, blocks, acc):
    def step(j, carry):
        m = lo + 2 * j
        e0, e1 = entries[m], entries[m + 1]

        def product(e, m):
            at = pl.multiple_of(((e >> 8) & 15) * 128, 128)
            return jnp.dot(
                tiles[m], blocks[pl.ds(at, 128), :], preferred_element_type=jnp.float32
            )

        p0, p1 = product(e0, m), product(e1, m + 1)
        acc[e0 >> 12] += p0
        acc[e1 >> 12] += p1
        return carry

    lax.fori_loop(0, (hi - lo) // 2, step, 0)


def early_kernel(groups, entries, starts, tiles, *refs):
    arrays, acc = refs[:groups], refs[groups]
    acc[...] = jnp.zeros_like(acc)
    for g in range(groups):
        add_group(entries, starts[g], starts[g + 1], tiles, arrays[g], acc)


def late_kernel(first, groups, entries, starts, tiles, acc_in, *refs):
    arrays, (keep, give, acc) = refs[:groups], refs[groups:]
    acc[...] = acc_in[...]
    for g in range(groups):
        add_group(entries, starts[first + g], starts[first + g + 1], tiles, arrays[g], acc)
    half = keep.shape[0]
    keep[...] = acc[:half]
    give[...] = acc[half : 2 * half]


def whole(space):
    return pl.BlockSpec(memory_space=space)


def add_early(entries, starts, tiles, arrays, row_blocks):
    width = arrays[0].shape[1]
    return pl.pallas_call(
        functools.partial(early_kernel, len(arrays)),
        out_shape=VMEM((row_blocks + 1, 128, width), jnp.float32),
        in_specs=[whole(SMEM)] * 2 + [whole(VMEM)] * (1 + len(arrays)),
        out_specs=whole(VMEM),
        name="add_early",
        compiler_params=pltpu.CompilerParams(vmem_limit_bytes=4 << 20),
        cost_estimate=pl.CostEstimate(flops=1 << 28, bytes_accessed=4 << 20, transcendentals=0),
    )(entries, starts, tiles, *arrays)


def add_late(entries, starts, tiles, acc, arrays, first):
    blocks, size, width = acc.shape
    half = VMEM(((blocks - 1) // 2, size, width), jnp.float32)
    return pl.pallas_call(
        functools.partial(late_kernel, first, len(arrays)),
        out_shape=(half, half),
        in_specs=[whole(SMEM)] * 2 + [whole(VMEM)] * (2 + len(arrays)),
        out_specs=(whole(VMEM), whole(VMEM)),
        scratch_shapes=[VMEM(acc.shape, jnp.float32)],
        name="add_late",
        compiler_params=pltpu.CompilerParams(vmem_limit_bytes=8 << 20),
        cost_estimate=pl.CostEstimate(flops=1 << 25, bytes_accessed=2 << 20, transcendentals=0),
    )(entries, starts, tiles, acc, *arrays)


def dense_kernel(core, mine, theirs, weight, bias, grad_out, output, keep, give, full):
    hidden = (mine[...] + theirs[...]).reshape(grad_out.shape).astype(jnp.bfloat16)
    pre_act = jnp.dot(hidden, weight[...], preferred_element_type=jnp.float32) + bias[...]
    sigma = 1.0 / (1.0 + jnp.exp(-pre_act))
    output[...] = (pre_act * sigma).astype(jnp.bfloat16)
    grad_pre = grad_out[...].astype(jnp.float32) * sigma * (1.0 + pre_act * (1.0 - sigma))
    grad_low = grad_pre.astype(jnp.bfloat16)
    full[...] = lax.dot_general(
        hidden, grad_low, (((0,), (0,)), ((), ())), preferred_element_type=jnp.float32
    )
    sums = jnp.sum(grad_pre, axis=0, keepdims=True)
    sums = jnp.broadcast_to(sums, (8, sums.shape[1]))
    share = full.shape[0] // 2
    at = core[0]
    keep[:share] = full[pl.ds(pl.multiple_of(at * share, share), share), :]
    give[:share] = full[pl.ds(pl.multiple_of((1 - at) * share, share), share), :]
    keep[share:] = sums
    give[share:] = sums


def dense(core, mine, theirs, weight, bias, grad_out):
    width = weight.shape[0]
    part = VMEM((width // 2 + 8, width), jnp.float32)
    return pl.pallas_call(
        dense_kernel,
        out_shape=(jax.ShapeDtypeStruct(grad_out.shape, jnp.bfloat16), part, part),
        in_specs=[whole(SMEM)] + [whole(VMEM)] * 5,
        out_specs=(whole(VMEM),) * 3,
        scratch_shapes=[VMEM((width, width), jnp.float32)],
        name="dense",
        compiler_params=pltpu.CompilerParams(vmem_limit_bytes=16 << 20),
        cost_estimate=pl.CostEstimate(
            flops=1 << 27, bytes_accessed=2 << 20, transcendentals=1 << 17
        ),
    )(core.reshape(1), mine, theirs, weight, bias.reshape(1, width), grad_out)


def shards(features, adj_tiles, tile_index, weight, bias_vec, grad_out):
    core = lax.axis_index("replica")
    row_blocks = 2 * features.shape[0] // adj_tiles.shape[1]
    slots = adj_tiles.shape[0] // 8

    z1 = along_z(features, 1, "z1")
    r0 = first_hop(features, "r0")
    z2 = along_z(features, 2, "z2")
    z3 = along_z(features, 3, "z3")
    other_tiles = swap(adj_tiles, "tiles")
    other_index = swap(tile_index, "index")
    entries, starts = work_list(tile_index, other_index, slots, row_blocks)
    tiles = gather_tiles(entries, starts, adj_tiles, other_tiles)

    arrays = []
    for k, (own, near) in enumerate(((features, r0), (z1, None), (z2, None), (z3, None))):
        if near is None:
            near = first_hop(own, f"r{k}")
        pair = jnp.concatenate([own, near], axis=0)
        arrays += [pair, second_hop(pair, f"q{k}")]

    acc = add_early(entries, starts, tiles, arrays[:7], row_blocks)
    mine, give = add_late(entries, starts, tiles, acc, arrays[7:], 7)
    theirs = swap(give, "rows")
    output, keep, give = dense(core, mine, theirs, weight, bias_vec, grad_out)
    part = keep + swap(give, "halves")
    part = part + first_hop(part, "sum1")
    part = part + second_hop(part, "sum2")
    part = part + along_z(part, 1, "sum3")
    part = part + along_z(part, 2, "sum4")
    rest = swap(part, "back")
    share = part.shape[0] - 8
    top = jnp.where(core == 0, part, rest)
    low = jnp.where(core == 0, rest, part)
    grad_weight = jnp.concatenate([top[:share], low[:share]], axis=0)
    return output, grad_weight, top[share]


def solution(mesh):
    placed = (
        P(BOTH, None),
        P(BOTH, None, None),
        P(BOTH, None),
        P(),
        P(),
        P(BOTH, None),
    )
    small = mesh.shape["section"] == 16 and mesh.shape["replica"] == 2
    return jax.shard_map(
        shards if small else general_shards,
        mesh=mesh,
        in_specs=placed,
        out_specs=(P(BOTH, None), P(), P()),
        check_vma=False,
    )
```

```python
import functools

import jax
import jax.numpy as jnp
from jax import lax
from jax.experimental import pallas as pl
from jax.experimental.pallas import tpu as pltpu
from jax.sharding import PartitionSpec as P

BOTH = ("section", "replica")
VMEM = pltpu.VMEM
SMEM = pltpu.SMEM


def spread(x, axis, root):
    mine = lax.axis_index(axis) == root
    return lax.psum(jnp.where(mine, x, jnp.zeros_like(x)), axis)


def add_tiles(summed, received, adj_tiles, row_ids, col_ids, first_slot, count, levels):
    tile_part = lax.dynamic_slice_in_dim(adj_tiles, first_slot, count, 0)
    row_pick = lax.dynamic_slice_in_dim(row_ids, first_slot, count, 0)
    col_pick = lax.dynamic_slice_in_dim(col_ids, first_slot, count, 0)
    picked = received[col_pick]
    products = jnp.einsum("kab,kbd->kad", tile_part, picked, preferred_element_type=jnp.float32)
    onehot = (row_pick[:, None] == levels[None, :]).astype(jnp.float32)
    return summed + jnp.einsum("kr,kad->rad", onehot, products, precision=lax.Precision.HIGHEST)


def general_shards(features, adj_tiles, tile_index, weight, bias_vec, grad_out):
    replicas = lax.axis_size("replica")
    replica_idx = lax.axis_index("replica")
    own_slab = lax.all_gather(features, "replica", axis=0, tiled=True)
    rows_slab, feat_width = own_slab.shape
    block_size = adj_tiles.shape[1]
    row_blocks = rows_slab // block_size
    turn_count = lax.axis_size("section") // replicas
    slot_count = adj_tiles.shape[0] // turn_count
    row_ids = tile_index[:, 0]
    col_ids = tile_index[:, 1]
    levels = jnp.arange(row_blocks, dtype=jnp.int32)

    def turn_step(step_idx, summed):
        received = spread(own_slab, "section", replica_idx * turn_count + step_idx)
        received = received.reshape(row_blocks, block_size, feat_width)
        first_slot = step_idx * slot_count
        return add_tiles(
            summed, received, adj_tiles, row_ids, col_ids, first_slot, slot_count, levels
        )

    start_sum = jnp.zeros((row_blocks, block_size, feat_width), jnp.float32)
    partial_sum = lax.fori_loop(0, turn_count, turn_step, start_sum).reshape(rows_slab, feat_width)
    share = rows_slab // replicas
    whole_sum = lax.psum(partial_sum, "replica")
    local_rows = lax.dynamic_slice_in_dim(whole_sum, replica_idx * share, share, 0)
    hidden = local_rows.astype(jnp.bfloat16)
    pre_act = jnp.dot(hidden, weight, preferred_element_type=jnp.float32) + bias_vec
    output = jax.nn.silu(pre_act).astype(jnp.bfloat16)
    sigma = jax.nn.sigmoid(pre_act)
    grad_pre = grad_out.astype(jnp.float32) * sigma * (1.0 + pre_act * (1.0 - sigma))
    grad_low = grad_pre.astype(jnp.bfloat16)
    weight_term = jnp.einsum("nd,ne->de", hidden, grad_low, preferred_element_type=jnp.float32)
    grad_weight, grad_bias = lax.psum((weight_term, jnp.sum(grad_pre, axis=0)), BOTH)
    return (output, grad_weight, grad_bias)


def send(x, target, name):
    perm = [(2 * p + c, 2 * target(p, c) + c) for p in range(16) for c in range(2)]
    with jax.named_scope(name):
        return lax.ppermute(x, BOTH, perm)


def swap(x, name):
    with jax.named_scope(name):
        return lax.ppermute(x, "replica", [(0, 1), (1, 0)])


def first_hop(x, name):
    return send(x, lambda p, c: p ^ (1 if c == 0 else 2), name)


def second_hop(x, name):
    return send(x, lambda p, c: p ^ (2 if c == 0 else 1), name)


def diagonal(x, name):
    return send(x, lambda p, c: p ^ 3, name)


def along_z(x, k, name):
    return send(x, lambda p, c: p ^ (4 * k), name)


def join(own, near):
    return jnp.concatenate([own, near], axis=0)


def after(*arrays):
    return lax.optimization_barrier(arrays)


def work_list(index, slots, row_blocks):
    chip = lax.axis_index("section")
    core = lax.axis_index("replica")
    half = row_blocks // 2
    count = index.shape[0] // 2
    tile = jnp.arange(2 * count, dtype=jnp.int32)
    source = tile // slots
    row, col = index[:, 0], index[:, 1]
    live = (row >= 0) & (col // half == core)
    apart = source ^ chip
    x_apart, y_apart, z_apart = apart & 1, (apart >> 1) & 1, apart >> 2
    near = jnp.where(core == 0, x_apart, y_apart)
    far = jnp.where(core == 0, y_apart, x_apart)
    groups = 8
    group = jnp.where(live, 2 * z_apart + far, groups)
    block = half * near + col % half
    mine = tile // count == core
    entry = (tile % count + jnp.where(mine, 0, count)) | (block << 8) | ((row ^ (half * core)) << 12)
    spare = row_blocks << 12
    sizes = jnp.sum((group[:, None] == jnp.arange(groups)[None, :]).astype(jnp.int32), axis=0)
    padded = (sizes + 1) // 2 * 2
    edge = jnp.arange(groups + 1)
    starts = jnp.sum(jnp.where(edge[None, :groups] < edge[:, None], padded[None, :], 0), axis=1)
    same = (group[:, None] == group[None, :]) & (tile[None, :] < tile[:, None])
    rank = jnp.sum(same.astype(jnp.int32), axis=1)
    base = jnp.sum(jnp.where(group[:, None] == edge[None, :groups], starts[None, :groups], 0), axis=1)
    place = jnp.where(live, base + rank, -1)
    length = 2 * count + 2 * groups
    hit = place[None, :] == jnp.arange(length, dtype=jnp.int32)[:, None]
    entries = spare + jnp.sum(jnp.where(hit, (entry - spare)[None, :], 0), axis=1)
    return entries, starts


def gather_kernel(count, entries, starts, own, other, out, sem):
    total = starts[8]

    def begin(m, carry):
        tile = entries[m] & 255

        @pl.when(tile < count)
        def _():
            pltpu.make_async_copy(own.at[tile], out.at[m], sem).start()

        @pl.when(tile >= count)
        def _():
            pltpu.make_async_copy(other.at[tile - count], out.at[m], sem).start()

        return carry

    def finish(m, carry):
        pltpu.make_async_copy(own.at[0], out.at[0], sem).wait()
        return carry

    lax.fori_loop(0, total, begin, 0)
    lax.fori_loop(0, total, finish, 0)


def gather_tiles(entries, starts, own, other):
    size = own.shape[1]
    return pl.pallas_call(
        functools.partial(gather_kernel, own.shape[0]),
        out_shape=VMEM((entries.shape[0], size, size), own.dtype),
        in_specs=[pl.BlockSpec(memory_space=SMEM)] * 2 + [pl.BlockSpec(memory_space=pltpu.HBM)] * 2,
        out_specs=pl.BlockSpec(memory_space=VMEM),
        scratch_shapes=[pltpu.SemaphoreType.DMA],
        name="gather_tiles",
        compiler_params=pltpu.CompilerParams(vmem_limit_bytes=1 << 20),
        cost_estimate=pl.CostEstimate(flops=4000000000, bytes_accessed=10000000, transcendentals=0),
    )(entries, starts, own, other)


def add_group(entries, lo, hi, tiles, blocks, acc):
    def step(j, carry):
        m = lo + 2 * j
        e0, e1 = entries[m], entries[m + 1]

        def product(e, m):
            at = pl.multiple_of(((e >> 8) & 15) * 128, 128)
            return jnp.dot(
                tiles[m], blocks[pl.ds(at, 128), :], preferred_element_type=jnp.float32
            )

        p0, p1 = product(e0, m), product(e1, m + 1)
        acc[e0 >> 12] += p0
        acc[e1 >> 12] += p1
        return carry

    lax.fori_loop(0, (hi - lo) // 2, step, 0)


def add_kernel(groups, fresh, entries, starts, tiles, *refs):
    arrays, acc = refs[: len(groups)], refs[-1]
    if fresh:
        acc[...] = jnp.zeros_like(acc)
    for g, array in zip(groups, arrays):
        add_group(entries, starts[g], starts[g + 1], tiles, array, acc)


def late_kernel(groups, entries, starts, tiles, *refs):
    arrays, (acc, keep, give) = refs[: len(groups)], refs[len(groups) + 1 :]
    for g, array in zip(groups, arrays):
        add_group(entries, starts[g], starts[g + 1], tiles, array, acc)
    half = keep.shape[0]
    keep[...] = acc[:half]
    give[...] = acc[half : 2 * half]


def whole(space):
    return pl.BlockSpec(memory_space=space)


def add_groups(work, arrays, groups, acc, row_blocks, name, cost=4000000000):
    entries, starts, tiles = work
    shape = VMEM((row_blocks + 1, 128, arrays[0].shape[1]), jnp.float32)
    fresh = acc is None
    return pl.pallas_call(
        functools.partial(add_kernel, groups, fresh),
        out_shape=shape,
        in_specs=[whole(SMEM)] * 2 + [whole(VMEM)] * (1 + len(arrays) + (not fresh)),
        out_specs=whole(VMEM),
        name=name,
        input_output_aliases={} if fresh else {3 + len(arrays): 0},
        compiler_params=pltpu.CompilerParams(vmem_limit_bytes=4 << 20),
        cost_estimate=pl.CostEstimate(flops=cost, bytes_accessed=cost // 400, transcendentals=0),
    )(entries, starts, tiles, *arrays, *([] if fresh else [acc]))


def add_late(work, arrays, groups, acc, row_blocks):
    entries, starts, tiles = work
    half = VMEM((row_blocks // 2, 128, arrays[0].shape[1]), jnp.float32)
    return pl.pallas_call(
        functools.partial(late_kernel, groups),
        out_shape=(VMEM(acc.shape, jnp.float32), half, half),
        in_specs=[whole(SMEM)] * 2 + [whole(VMEM)] * (2 + len(arrays)),
        out_specs=(whole(VMEM),) * 3,
        name="add_late",
        input_output_aliases={3 + len(arrays): 0},
        compiler_params=pltpu.CompilerParams(vmem_limit_bytes=4 << 20),
        cost_estimate=pl.CostEstimate(flops=1 << 25, bytes_accessed=2 << 20, transcendentals=0),
    )(entries, starts, tiles, *arrays, acc)[1:]


def dense_kernel(core, mine, theirs, weight, bias, grad_out, output, keep, give, full):
    hidden = (mine[...] + theirs[...]).reshape(grad_out.shape).astype(jnp.bfloat16)
    pre_act = jnp.dot(hidden, weight[...], preferred_element_type=jnp.float32) + bias[...]
    sigma = 1.0 / (1.0 + jnp.exp(-pre_act))
    output[...] = (pre_act * sigma).astype(jnp.bfloat16)
    grad_pre = grad_out[...].astype(jnp.float32) * sigma * (1.0 + pre_act * (1.0 - sigma))
    grad_low = grad_pre.astype(jnp.bfloat16)
    full[...] = lax.dot_general(
        hidden, grad_low, (((0,), (0,)), ((), ())), preferred_element_type=jnp.float32
    )
    sums = jnp.sum(grad_pre, axis=0, keepdims=True)
    sums = jnp.broadcast_to(sums, (8, sums.shape[1]))
    share = full.shape[0] // 2
    at = core[0]
    keep[:share] = full[pl.ds(pl.multiple_of(at * share, share), share), :]
    give[:share] = full[pl.ds(pl.multiple_of((1 - at) * share, share), share), :]
    keep[share:] = sums
    give[share:] = sums


def dense(core, mine, theirs, weight, bias, grad_out):
    width = weight.shape[0]
    part = VMEM((width // 2 + 8, width), jnp.float32)
    return pl.pallas_call(
        dense_kernel,
        out_shape=(jax.ShapeDtypeStruct(grad_out.shape, jnp.bfloat16), part, part),
        in_specs=[whole(SMEM)] + [whole(VMEM)] * 5,
        out_specs=(whole(VMEM),) * 3,
        scratch_shapes=[VMEM((width, width), jnp.float32)],
        name="dense",
        compiler_params=pltpu.CompilerParams(vmem_limit_bytes=16 << 20),
        cost_estimate=pl.CostEstimate(
            flops=1 << 27, bytes_accessed=2 << 20, transcendentals=1 << 17
        ),
    )(core.reshape(1), mine, theirs, weight, bias.reshape(1, width), grad_out)


def shards(features, adj_tiles, tile_index, weight, bias_vec, grad_out):
    core = lax.axis_index("replica")
    row_blocks = 2 * features.shape[0] // adj_tiles.shape[1]
    slots = adj_tiles.shape[0] // 8

    index = lax.all_gather(tile_index, "replica", axis=0, tiled=True)
    z1 = along_z(features, 1, "z1")
    z2 = along_z(features, 2, "z2")
    r0 = first_hop(features, "r0")
    pair0 = join(features, r0)
    q0 = second_hop(pair0, "q0")
    again = features
    tiles_in = adj_tiles
    z1, again = after(z1, features)
    z3 = along_z(again, 3, "z3")
    other_tiles = swap(tiles_in, "tiles")
    entries, starts = work_list(index, slots, row_blocks)
    tiles = gather_tiles(entries, starts, adj_tiles, other_tiles)
    pair1 = join(z1, first_hop(z1, "r1"))
    q1 = second_hop(pair1, "q1")
    pair2 = join(z2, first_hop(z2, "r2"))
    q2 = second_hop(pair2, "q2")
    work = (entries, starts, tiles)
    acc = add_groups(work, (pair0, q0, pair1), (0, 1, 2), None, row_blocks, "add_a")
    pair3 = join(z3, first_hop(z3, "r3"))
    q3 = second_hop(pair3, "q3")
    acc = add_groups(work, (q1, pair2), (3, 4), acc, row_blocks, "add_b")
    acc = add_groups(work, (q2, pair3), (5, 6), acc, row_blocks, "add_c")
    mine, give = add_late(work, (q3,), (7,), acc, row_blocks)
    theirs = swap(give, "rows")
    output, keep, give = dense(core, mine, theirs, weight, bias_vec, grad_out)
    part = keep + swap(give, "halves")
    part = part + first_hop(part, "sum1")
    part = part + second_hop(part, "sum2")
    low_part = part.astype(jnp.bfloat16)
    z_parts = [lax.reduce_precision(part, 8, 7)]
    z_parts += [along_z(low_part, k, f"sum{2 + k}").astype(jnp.float32) for k in (1, 2, 3)]
    part = (z_parts[0] + z_parts[1]) + (z_parts[2] + z_parts[3])
    rest = swap(part, "back")
    share = part.shape[0] - 8
    top = jnp.where(core == 0, part, rest)
    low = jnp.where(core == 0, rest, part)
    grad_weight = jnp.concatenate([top[:share], low[:share]], axis=0)
    return output, grad_weight, top[share]


def solution(mesh):
    placed = (
        P(BOTH, None),
        P(BOTH, None, None),
        P(BOTH, None),
        P(),
        P(),
        P(BOTH, None),
    )
    small = mesh.shape["section"] == 16 and mesh.shape["replica"] == 2
    return jax.shard_map(
        shards if small else general_shards,
        mesh=mesh,
        in_specs=placed,
        out_specs=(P(BOTH, None), P(), P()),
        check_vma=False,
    )
```

```python
import functools

import jax
import jax.numpy as jnp
from jax import lax
from jax.experimental import pallas as pl
from jax.experimental.pallas import tpu as pltpu
from jax.sharding import PartitionSpec as P

BOTH = ("section", "replica")
VMEM = pltpu.VMEM
SMEM = pltpu.SMEM


def spread(x, axis, root):
    mine = lax.axis_index(axis) == root
    return lax.psum(jnp.where(mine, x, jnp.zeros_like(x)), axis)


def add_tiles(summed, received, adj_tiles, row_ids, col_ids, first_slot, count, levels):
    tile_part = lax.dynamic_slice_in_dim(adj_tiles, first_slot, count, 0)
    row_pick = lax.dynamic_slice_in_dim(row_ids, first_slot, count, 0)
    col_pick = lax.dynamic_slice_in_dim(col_ids, first_slot, count, 0)
    picked = received[col_pick]
    products = jnp.einsum("kab,kbd->kad", tile_part, picked, preferred_element_type=jnp.float32)
    onehot = (row_pick[:, None] == levels[None, :]).astype(jnp.float32)
    return summed + jnp.einsum("kr,kad->rad", onehot, products, precision=lax.Precision.HIGHEST)


def general_shards(features, adj_tiles, tile_index, weight, bias_vec, grad_out):
    replicas = lax.axis_size("replica")
    replica_idx = lax.axis_index("replica")
    own_slab = lax.all_gather(features, "replica", axis=0, tiled=True)
    rows_slab, feat_width = own_slab.shape
    block_size = adj_tiles.shape[1]
    row_blocks = rows_slab // block_size
    turn_count = lax.axis_size("section") // replicas
    slot_count = adj_tiles.shape[0] // turn_count
    row_ids = tile_index[:, 0]
    col_ids = tile_index[:, 1]
    levels = jnp.arange(row_blocks, dtype=jnp.int32)

    def turn_step(step_idx, summed):
        received = spread(own_slab, "section", replica_idx * turn_count + step_idx)
        received = received.reshape(row_blocks, block_size, feat_width)
        first_slot = step_idx * slot_count
        return add_tiles(
            summed, received, adj_tiles, row_ids, col_ids, first_slot, slot_count, levels
        )

    start_sum = jnp.zeros((row_blocks, block_size, feat_width), jnp.float32)
    partial_sum = lax.fori_loop(0, turn_count, turn_step, start_sum).reshape(rows_slab, feat_width)
    share = rows_slab // replicas
    whole_sum = lax.psum(partial_sum, "replica")
    local_rows = lax.dynamic_slice_in_dim(whole_sum, replica_idx * share, share, 0)
    hidden = local_rows.astype(jnp.bfloat16)
    pre_act = jnp.dot(hidden, weight, preferred_element_type=jnp.float32) + bias_vec
    output = jax.nn.silu(pre_act).astype(jnp.bfloat16)
    sigma = jax.nn.sigmoid(pre_act)
    grad_pre = grad_out.astype(jnp.float32) * sigma * (1.0 + pre_act * (1.0 - sigma))
    grad_low = grad_pre.astype(jnp.bfloat16)
    weight_term = jnp.einsum("nd,ne->de", hidden, grad_low, preferred_element_type=jnp.float32)
    grad_weight, grad_bias = lax.psum((weight_term, jnp.sum(grad_pre, axis=0)), BOTH)
    return (output, grad_weight, grad_bias)


def send(x, target, name):
    perm = [(2 * p + c, 2 * target(p, c) + c) for p in range(16) for c in range(2)]
    with jax.named_scope(name):
        return lax.ppermute(x, BOTH, perm)


def swap(x, name):
    with jax.named_scope(name):
        return lax.ppermute(x, "replica", [(0, 1), (1, 0)])


def first_hop(x, name):
    return send(x, lambda p, c: p ^ (1 if c == 0 else 2), name)


def second_hop(x, name):
    return send(x, lambda p, c: p ^ (2 if c == 0 else 1), name)


def diagonal(x, name):
    return send(x, lambda p, c: p ^ 3, name)


def along_z(x, k, name):
    return send(x, lambda p, c: p ^ (4 * k), name)


def join(own, near):
    return jnp.concatenate([own, near], axis=0)


def after(*arrays):
    return lax.optimization_barrier(arrays)


def work_list(index, slots, row_blocks):
    chip = lax.axis_index("section")
    core = lax.axis_index("replica")
    half = row_blocks // 2
    count = index.shape[0] // 2
    tile = jnp.arange(2 * count, dtype=jnp.int32)
    source = tile // slots
    row, col = index[:, 0], index[:, 1]
    live = (row >= 0) & (col // half == core)
    apart = source ^ chip
    x_apart, y_apart, z_apart = apart & 1, (apart >> 1) & 1, apart >> 2
    near = jnp.where(core == 0, x_apart, y_apart)
    far = jnp.where(core == 0, y_apart, x_apart)
    groups = 8
    group = jnp.where(live, 2 * z_apart + far, groups)
    block = half * near + col % half
    mine = tile // count == core
    entry = (tile % count + jnp.where(mine, 0, count)) | (block << 8) | ((row ^ (half * core)) << 12)
    spare = row_blocks << 12
    sizes = jnp.sum((group[:, None] == jnp.arange(groups)[None, :]).astype(jnp.int32), axis=0)
    padded = (sizes + 1) // 2 * 2
    edge = jnp.arange(groups + 1)
    starts = jnp.sum(jnp.where(edge[None, :groups] < edge[:, None], padded[None, :], 0), axis=1)
    same = (group[:, None] == group[None, :]) & (tile[None, :] < tile[:, None])
    rank = jnp.sum(same.astype(jnp.int32), axis=1)
    base = jnp.sum(jnp.where(group[:, None] == edge[None, :groups], starts[None, :groups], 0), axis=1)
    place = jnp.where(live, base + rank, -1)
    length = 2 * count + 2 * groups
    hit = place[None, :] == jnp.arange(length, dtype=jnp.int32)[:, None]
    entries = spare + jnp.sum(jnp.where(hit, (entry - spare)[None, :], 0), axis=1)
    return entries, starts


def gather_kernel(count, entries, starts, own, other, out, sem):
    pairs = starts[8] // 2

    def fetch(m):
        tile = entries[m] & 255

        @pl.when(tile < count)
        def _():
            pltpu.make_async_copy(own.at[tile], out.at[m], sem).start()

        @pl.when(tile >= count)
        def _():
            pltpu.make_async_copy(other.at[tile - count], out.at[m], sem).start()

    def begin(j, carry):
        fetch(2 * j)
        fetch(2 * j + 1)
        return carry

    def finish(size):
        def step(j, carry):
            block = out.at[pl.ds(0, size)]
            pltpu.make_async_copy(own.at[pl.ds(0, size)], block, sem).wait()
            return carry

        return step

    lax.fori_loop(0, pairs, begin, 0)
    lax.fori_loop(0, pairs // 8, finish(16), 0)
    lax.fori_loop(0, pairs % 8, finish(2), 0)


def gather_tiles(entries, starts, own, other):
    size = own.shape[1]
    return pl.pallas_call(
        functools.partial(gather_kernel, own.shape[0]),
        out_shape=VMEM((entries.shape[0], size, size), own.dtype),
        in_specs=[pl.BlockSpec(memory_space=SMEM)] * 2 + [pl.BlockSpec(memory_space=pltpu.HBM)] * 2,
        out_specs=pl.BlockSpec(memory_space=VMEM),
        scratch_shapes=[pltpu.SemaphoreType.DMA],
        name="gather_tiles",
        compiler_params=pltpu.CompilerParams(vmem_limit_bytes=47 << 20),
        cost_estimate=pl.CostEstimate(flops=0, bytes_accessed=1 << 10, transcendentals=0),
    )(entries, starts, own, other)


def add_group(entries, lo, hi, tiles, blocks, acc):
    def step(j, carry):
        m = lo + 2 * j
        e0, e1 = entries[m], entries[m + 1]

        def product(e, m):
            at = pl.multiple_of(((e >> 8) & 15) * 128, 128)
            return jnp.dot(
                tiles[m], blocks[pl.ds(at, 128), :], preferred_element_type=jnp.float32
            )

        p0, p1 = product(e0, m), product(e1, m + 1)
        acc[e0 >> 12] += p0
        acc[e1 >> 12] += p1
        return carry

    lax.fori_loop(0, (hi - lo) // 2, step, 0)


def add_kernel(groups, fresh, entries, starts, tiles, *refs):
    arrays, acc = refs[: len(groups)], refs[-1]
    if fresh:
        acc[...] = jnp.zeros_like(acc)
    for g, array in zip(groups, arrays):
        add_group(entries, starts[g], starts[g + 1], tiles, array, acc)


def late_kernel(groups, entries, starts, tiles, *refs):
    arrays, (acc, give) = refs[: len(groups)], refs[len(groups) + 1 :]
    for g, array in zip(groups, arrays):
        add_group(entries, starts[g], starts[g + 1], tiles, array, acc)
    half = give.shape[0]
    give[...] = acc[half : 2 * half]


def whole(space):
    return pl.BlockSpec(memory_space=space)


def add_groups(work, arrays, groups, acc, row_blocks, name):
    entries, starts, tiles = work
    shape = VMEM((row_blocks + 1, 128, arrays[0].shape[1]), jnp.float32)
    fresh = acc is None
    return pl.pallas_call(
        functools.partial(add_kernel, groups, fresh),
        out_shape=shape,
        in_specs=[whole(SMEM)] * 2 + [whole(VMEM)] * (1 + len(arrays) + (not fresh)),
        out_specs=whole(VMEM),
        name=name,
        input_output_aliases={} if fresh else {3 + len(arrays): 0},
        compiler_params=pltpu.CompilerParams(vmem_limit_bytes=4 << 20),
        cost_estimate=pl.CostEstimate(flops=16 << 28, bytes_accessed=4 << 20, transcendentals=0),
    )(entries, starts, tiles, *arrays, *([] if fresh else [acc]))


def add_late(work, arrays, groups, acc, row_blocks):
    entries, starts, tiles = work
    half = VMEM((row_blocks // 2, 128, arrays[0].shape[1]), jnp.float32)
    return pl.pallas_call(
        functools.partial(late_kernel, groups),
        out_shape=(VMEM(acc.shape, jnp.float32), half),
        in_specs=[whole(SMEM)] * 2 + [whole(VMEM)] * (2 + len(arrays)),
        out_specs=(whole(VMEM),) * 2,
        name="add_late",
        input_output_aliases={3 + len(arrays): 0},
        compiler_params=pltpu.CompilerParams(vmem_limit_bytes=4 << 20),
        cost_estimate=pl.CostEstimate(flops=1 << 25, bytes_accessed=2 << 20, transcendentals=0),
    )(entries, starts, tiles, *arrays, acc)


def dense_kernel(core, mine, theirs, weight, bias, grad_out, output, keep, give, full):
    hidden = (mine[: theirs.shape[0]] + theirs[...]).reshape(grad_out.shape).astype(jnp.bfloat16)
    pre_act = jnp.dot(hidden, weight[...], preferred_element_type=jnp.float32) + bias[...]
    sigma = 1.0 / (1.0 + jnp.exp(-pre_act))
    output[...] = (pre_act * sigma).astype(jnp.bfloat16)
    grad_pre = grad_out[...].astype(jnp.float32) * sigma * (1.0 + pre_act * (1.0 - sigma))
    grad_low = grad_pre.astype(jnp.bfloat16)
    full[...] = lax.dot_general(
        hidden, grad_low, (((0,), (0,)), ((), ())), preferred_element_type=jnp.float32
    )
    sums = jnp.sum(grad_pre, axis=0, keepdims=True)
    sums = jnp.broadcast_to(sums, (8, sums.shape[1]))
    share = full.shape[0] // 2
    at = core[0]
    keep[:share] = full[pl.ds(pl.multiple_of(at * share, share), share), :]
    give[:share] = full[pl.ds(pl.multiple_of((1 - at) * share, share), share), :]
    keep[share:] = sums
    give[share:] = sums


def dense(core, mine, theirs, weight, bias, grad_out):
    width = weight.shape[0]
    part = VMEM((width // 2 + 8, width), jnp.float32)
    return pl.pallas_call(
        dense_kernel,
        out_shape=(jax.ShapeDtypeStruct(grad_out.shape, jnp.bfloat16), part, part),
        in_specs=[whole(SMEM)] + [whole(VMEM)] * 5,
        out_specs=(whole(VMEM),) * 3,
        scratch_shapes=[VMEM((width, width), jnp.float32)],
        name="dense",
        compiler_params=pltpu.CompilerParams(vmem_limit_bytes=16 << 20),
        cost_estimate=pl.CostEstimate(
            flops=1 << 27, bytes_accessed=2 << 20, transcendentals=1 << 17
        ),
    )(core.reshape(1), mine, theirs, weight, bias.reshape(1, width), grad_out)


def finish_kernel(core, part, rest, weight, bias):
    share = part.shape[0] - 8
    at = core[0]
    weight[pl.ds(pl.multiple_of(at * share, share), share), :] = part[:share]
    weight[pl.ds(pl.multiple_of((1 - at) * share, share), share), :] = rest[:share]

    @pl.when(at == 0)
    def _():
        bias[...] = part[pl.ds(share, 1), :]

    @pl.when(at != 0)
    def _():
        bias[...] = rest[pl.ds(share, 1), :]


def finish(core, part, rest):
    rows, width = part.shape
    return pl.pallas_call(
        finish_kernel,
        out_shape=(
            jax.ShapeDtypeStruct((2 * (rows - 8), width), jnp.float32),
            jax.ShapeDtypeStruct((1, width), jnp.float32),
        ),
        in_specs=[whole(SMEM)] + [whole(VMEM)] * 2,
        out_specs=(whole(VMEM),) * 2,
        name="finish",
        compiler_params=pltpu.CompilerParams(vmem_limit_bytes=4 << 20),
    )(core.reshape(1), part, rest)


def shards(features, adj_tiles, tile_index, weight, bias_vec, grad_out):
    core = lax.axis_index("replica")
    row_blocks = 2 * features.shape[0] // adj_tiles.shape[1]
    slots = adj_tiles.shape[0] // 8

    z1 = along_z(features, 1, "z1")
    z2 = along_z(features, 2, "z2")
    r0 = first_hop(features, "r0")
    r0, index = after(r0, tile_index)
    index = lax.all_gather(index, "replica", axis=0, tiled=True)
    pair0 = join(features, r0)
    q0 = second_hop(pair0, "q0")
    other_tiles = swap(adj_tiles, "tiles")
    z1, again = after(z1, features)
    z3 = along_z(again, 3, "z3")
    pair1 = join(z1, first_hop(z1, "r1"))
    q1 = along_z(q0, 1, "q1")
    z2, q0, other_tiles = after(z2, q0, other_tiles)
    pair2 = join(z2, first_hop(z2, "r2"))
    pair2, other_tiles = after(pair2, other_tiles)
    q2 = second_hop(pair2, "q2")
    z3, pair1, pair2 = after(z3, pair1, pair2)
    pair3 = join(z3, first_hop(z3, "r3"))
    q3 = second_hop(pair3, "q3")
    entries, starts = work_list(index, slots, row_blocks)
    tiles = gather_tiles(entries, starts, adj_tiles, other_tiles)
    work = (entries, starts, tiles)
    acc = add_groups(work, (pair0, q0, pair1), (0, 1, 2), None, row_blocks, "add_a")
    acc = add_groups(work, (q1, pair2), (3, 4), acc, row_blocks, "add_b")
    acc = add_groups(work, (q2, pair3), (5, 6), acc, row_blocks, "add_c")
    mine, give = add_late(work, (q3,), (7,), acc, row_blocks)
    theirs = swap(give, "rows")
    output, keep, give = dense(core, mine, theirs, weight, bias_vec, grad_out)
    part = keep + swap(give, "halves")
    part = part + first_hop(part, "sum1")
    part = part + second_hop(part, "sum2")
    low_part = part.astype(jnp.bfloat16)
    z_parts = [lax.reduce_precision(part, 8, 7)]
    z_parts += [along_z(low_part, k, f"sum{2 + k}").astype(jnp.float32) for k in (1, 2, 3)]
    part = (z_parts[0] + z_parts[1]) + (z_parts[2] + z_parts[3])
    rest = swap(part, "back")
    grad_weight, grad_bias = finish(core, part, rest)
    return output, grad_weight, grad_bias.reshape(bias_vec.shape)


def solution(mesh):
    placed = (
        P(BOTH, None),
        P(BOTH, None, None),
        P(BOTH, None),
        P(),
        P(),
        P(BOTH, None),
    )
    small = mesh.shape["section"] == 16 and mesh.shape["replica"] == 2
    return jax.shard_map(
        shards if small else general_shards,
        mesh=mesh,
        in_specs=placed,
        out_specs=(P(BOTH, None), P(), P()),
        check_vma=False,
    )
```

```python
import functools

import jax
import jax.numpy as jnp
from jax import lax
from jax.experimental import pallas as pl
from jax.experimental.pallas import tpu as pltpu
from jax.sharding import PartitionSpec as P

BOTH = ("section", "replica")
VMEM = pltpu.VMEM
SMEM = pltpu.SMEM


def spread(x, axis, root):
    mine = lax.axis_index(axis) == root
    return lax.psum(jnp.where(mine, x, jnp.zeros_like(x)), axis)


def add_tiles(summed, received, adj_tiles, row_ids, col_ids, first_slot, count, levels):
    tile_part = lax.dynamic_slice_in_dim(adj_tiles, first_slot, count, 0)
    row_pick = lax.dynamic_slice_in_dim(row_ids, first_slot, count, 0)
    col_pick = lax.dynamic_slice_in_dim(col_ids, first_slot, count, 0)
    picked = received[col_pick]
    products = jnp.einsum("kab,kbd->kad", tile_part, picked, preferred_element_type=jnp.float32)
    onehot = (row_pick[:, None] == levels[None, :]).astype(jnp.float32)
    return summed + jnp.einsum("kr,kad->rad", onehot, products, precision=lax.Precision.HIGHEST)


def general_shards(features, adj_tiles, tile_index, weight, bias_vec, grad_out):
    replicas = lax.axis_size("replica")
    replica_idx = lax.axis_index("replica")
    own_slab = lax.all_gather(features, "replica", axis=0, tiled=True)
    rows_slab, feat_width = own_slab.shape
    block_size = adj_tiles.shape[1]
    row_blocks = rows_slab // block_size
    turn_count = lax.axis_size("section") // replicas
    slot_count = adj_tiles.shape[0] // turn_count
    row_ids = tile_index[:, 0]
    col_ids = tile_index[:, 1]
    levels = jnp.arange(row_blocks, dtype=jnp.int32)

    def turn_step(step_idx, summed):
        received = spread(own_slab, "section", replica_idx * turn_count + step_idx)
        received = received.reshape(row_blocks, block_size, feat_width)
        first_slot = step_idx * slot_count
        return add_tiles(
            summed, received, adj_tiles, row_ids, col_ids, first_slot, slot_count, levels
        )

    start_sum = jnp.zeros((row_blocks, block_size, feat_width), jnp.float32)
    partial_sum = lax.fori_loop(0, turn_count, turn_step, start_sum).reshape(rows_slab, feat_width)
    share = rows_slab // replicas
    whole_sum = lax.psum(partial_sum, "replica")
    local_rows = lax.dynamic_slice_in_dim(whole_sum, replica_idx * share, share, 0)
    hidden = local_rows.astype(jnp.bfloat16)
    pre_act = jnp.dot(hidden, weight, preferred_element_type=jnp.float32) + bias_vec
    output = jax.nn.silu(pre_act).astype(jnp.bfloat16)
    sigma = jax.nn.sigmoid(pre_act)
    grad_pre = grad_out.astype(jnp.float32) * sigma * (1.0 + pre_act * (1.0 - sigma))
    grad_low = grad_pre.astype(jnp.bfloat16)
    weight_term = jnp.einsum("nd,ne->de", hidden, grad_low, preferred_element_type=jnp.float32)
    grad_weight, grad_bias = lax.psum((weight_term, jnp.sum(grad_pre, axis=0)), BOTH)
    return (output, grad_weight, grad_bias)


def send(x, target, name):
    perm = [(2 * p + c, 2 * target(p, c) + c) for p in range(16) for c in range(2)]
    with jax.named_scope(name):
        return lax.ppermute(x, BOTH, perm)


def swap(x, name):
    with jax.named_scope(name):
        return lax.ppermute(x, "replica", [(0, 1), (1, 0)])


def first_hop(x, name):
    return send(x, lambda p, c: p ^ (1 if c == 0 else 2), name)


def second_hop(x, name):
    return send(x, lambda p, c: p ^ (2 if c == 0 else 1), name)


def diagonal(x, name):
    return send(x, lambda p, c: p ^ 3, name)


def along_z(x, k, name):
    return send(x, lambda p, c: p ^ (4 * k), name)


def join(own, near):
    return jnp.concatenate([own, near], axis=0)


def after(*arrays):
    return lax.optimization_barrier(arrays)


def work_list(index, slots, row_blocks):
    chip = lax.axis_index("section")
    core = lax.axis_index("replica")
    half = row_blocks // 2
    count = index.shape[0] // 2
    tile = jnp.arange(2 * count, dtype=jnp.int32)
    source = tile // slots
    row, col = index[:, 0], index[:, 1]
    live = (row >= 0) & (col // half == core)
    apart = source ^ chip
    x_apart, y_apart, z_apart = apart & 1, (apart >> 1) & 1, apart >> 2
    near = jnp.where(core == 0, x_apart, y_apart)
    far = jnp.where(core == 0, y_apart, x_apart)
    groups = 8
    group = jnp.where(live, 2 * z_apart + far, groups)
    block = half * near + col % half
    mine = tile // count == core
    entry = (tile % count + jnp.where(mine, 0, count)) | (block << 8) | ((row ^ (half * core)) << 12)
    spare = row_blocks << 12
    sizes = jnp.sum((group[:, None] == jnp.arange(groups)[None, :]).astype(jnp.int32), axis=0)
    padded = (sizes + 1) // 2 * 2
    edge = jnp.arange(groups + 1)
    starts = jnp.sum(jnp.where(edge[None, :groups] < edge[:, None], padded[None, :], 0), axis=1)
    same = (group[:, None] == group[None, :]) & (tile[None, :] < tile[:, None])
    rank = jnp.sum(same.astype(jnp.int32), axis=1)
    base = jnp.sum(jnp.where(group[:, None] == edge[None, :groups], starts[None, :groups], 0), axis=1)
    place = jnp.where(live, base + rank, -1)
    length = 2 * count + 2 * groups
    hit = place[None, :] == jnp.arange(length, dtype=jnp.int32)[:, None]
    entries = spare + jnp.sum(jnp.where(hit, (entry - spare)[None, :], 0), axis=1)
    return entries, starts


def gather_kernel(count, entries, starts, own, other, out, sem):
    pairs = starts[8] // 2

    def fetch(m):
        tile = entries[m] & 255

        @pl.when(tile < count)
        def _():
            pltpu.make_async_copy(own.at[tile], out.at[m], sem).start()

        @pl.when(tile >= count)
        def _():
            pltpu.make_async_copy(other.at[tile - count], out.at[m], sem).start()

    def begin(j, carry):
        fetch(2 * j)
        fetch(2 * j + 1)
        return carry

    def finish(size):
        def step(j, carry):
            block = out.at[pl.ds(0, size)]
            pltpu.make_async_copy(own.at[pl.ds(0, size)], block, sem).wait()
            return carry

        return step

    lax.fori_loop(0, pairs, begin, 0)
    lax.fori_loop(0, pairs // 8, finish(16), 0)
    lax.fori_loop(0, pairs % 8, finish(2), 0)


def gather_tiles(entries, starts, own, other):
    size = own.shape[1]
    return pl.pallas_call(
        functools.partial(gather_kernel, own.shape[0]),
        out_shape=VMEM((entries.shape[0], size, size), own.dtype),
        in_specs=[pl.BlockSpec(memory_space=SMEM)] * 2 + [pl.BlockSpec(memory_space=pltpu.HBM)] * 2,
        out_specs=pl.BlockSpec(memory_space=VMEM),
        scratch_shapes=[pltpu.SemaphoreType.DMA],
        name="gather_tiles",
        compiler_params=pltpu.CompilerParams(vmem_limit_bytes=47 << 20),
        cost_estimate=pl.CostEstimate(flops=0, bytes_accessed=1 << 10, transcendentals=0),
    )(entries, starts, own, other)


def add_group(entries, lo, hi, tiles, blocks, acc):
    def product(m):
        at = pl.multiple_of(((entries[m] >> 8) & 15) * 128, 128)
        return jnp.dot(tiles[m], blocks[pl.ds(at, 128), :], preferred_element_type=jnp.float32)

    def add(first, count):
        products = [product(first + i) for i in range(count)]
        for i, p in enumerate(products):
            acc[entries[first + i] >> 12] += p

    def four(j, carry):
        add(lo + 4 * j, 4)
        return carry

    fours = (hi - lo) // 4
    lax.fori_loop(0, fours, four, 0)

    @pl.when((hi - lo) % 4 != 0)
    def _():
        add(lo + 4 * fours, 2)


def add_kernel(groups, fresh, entries, starts, tiles, *refs):
    arrays, acc = refs[: len(groups)], refs[-1]
    if fresh:
        acc[...] = jnp.zeros_like(acc)
    for g, array in zip(groups, arrays):
        add_group(entries, starts[g], starts[g + 1], tiles, array, acc)


def late_kernel(groups, entries, starts, tiles, *refs):
    arrays, (acc, give) = refs[: len(groups)], refs[len(groups) + 1 :]
    for g, array in zip(groups, arrays):
        add_group(entries, starts[g], starts[g + 1], tiles, array, acc)
    half = give.shape[0]
    give[...] = acc[half : 2 * half]


def whole(space):
    return pl.BlockSpec(memory_space=space)


def add_groups(work, arrays, groups, acc, row_blocks, name):
    entries, starts, tiles = work
    shape = VMEM((row_blocks + 1, 128, arrays[0].shape[1]), jnp.float32)
    fresh = acc is None
    return pl.pallas_call(
        functools.partial(add_kernel, groups, fresh),
        out_shape=shape,
        in_specs=[whole(SMEM)] * 2 + [whole(VMEM)] * (1 + len(arrays) + (not fresh)),
        out_specs=whole(VMEM),
        name=name,
        input_output_aliases={} if fresh else {3 + len(arrays): 0},
        compiler_params=pltpu.CompilerParams(vmem_limit_bytes=4 << 20),
        cost_estimate=pl.CostEstimate(flops=16 << 28, bytes_accessed=4 << 20, transcendentals=0),
    )(entries, starts, tiles, *arrays, *([] if fresh else [acc]))


def add_late(work, arrays, groups, acc, row_blocks):
    entries, starts, tiles = work
    half = VMEM((row_blocks // 2, 128, arrays[0].shape[1]), jnp.float32)
    return pl.pallas_call(
        functools.partial(late_kernel, groups),
        out_shape=(VMEM(acc.shape, jnp.float32), half),
        in_specs=[whole(SMEM)] * 2 + [whole(VMEM)] * (2 + len(arrays)),
        out_specs=(whole(VMEM),) * 2,
        name="add_late",
        input_output_aliases={3 + len(arrays): 0},
        compiler_params=pltpu.CompilerParams(vmem_limit_bytes=4 << 20),
        cost_estimate=pl.CostEstimate(flops=1 << 25, bytes_accessed=2 << 20, transcendentals=0),
    )(entries, starts, tiles, *arrays, acc)


def dense_kernel(core, mine, theirs, weight, bias, grad_out, output, keep, give, full):
    hidden = (mine[: theirs.shape[0]] + theirs[...]).reshape(grad_out.shape).astype(jnp.bfloat16)
    pre_act = jnp.dot(hidden, weight[...], preferred_element_type=jnp.float32) + bias[...]
    sigma = 1.0 / (1.0 + jnp.exp(-pre_act))
    output[...] = (pre_act * sigma).astype(jnp.bfloat16)
    grad_pre = grad_out[...].astype(jnp.float32) * sigma * (1.0 + pre_act * (1.0 - sigma))
    grad_low = grad_pre.astype(jnp.bfloat16)
    full[...] = lax.dot_general(
        hidden, grad_low, (((0,), (0,)), ((), ())), preferred_element_type=jnp.float32
    )
    sums = jnp.sum(grad_pre, axis=0, keepdims=True)
    sums = jnp.broadcast_to(sums, (8, sums.shape[1]))
    share = full.shape[0] // 2
    at = core[0]
    keep[:share] = full[pl.ds(pl.multiple_of(at * share, share), share), :]
    give[:share] = full[pl.ds(pl.multiple_of((1 - at) * share, share), share), :]
    keep[share:] = sums
    give[share:] = sums


def dense(core, mine, theirs, weight, bias, grad_out):
    width = weight.shape[0]
    part = VMEM((width // 2 + 8, width), jnp.float32)
    return pl.pallas_call(
        dense_kernel,
        out_shape=(jax.ShapeDtypeStruct(grad_out.shape, jnp.bfloat16), part, part),
        in_specs=[whole(SMEM)] + [whole(VMEM)] * 5,
        out_specs=(whole(VMEM),) * 3,
        scratch_shapes=[VMEM((width, width), jnp.float32)],
        name="dense",
        compiler_params=pltpu.CompilerParams(vmem_limit_bytes=16 << 20),
        cost_estimate=pl.CostEstimate(
            flops=1 << 27, bytes_accessed=2 << 20, transcendentals=1 << 17
        ),
    )(core.reshape(1), mine, theirs, weight, bias.reshape(1, width), grad_out)


def finish_kernel(core, part, rest, weight, bias):
    share = part.shape[0] - 8
    at = core[0]
    weight[pl.ds(pl.multiple_of(at * share, share), share), :] = part[:share]
    weight[pl.ds(pl.multiple_of((1 - at) * share, share), share), :] = rest[:share]

    @pl.when(at == 0)
    def _():
        bias[...] = part[pl.ds(share, 1), :]

    @pl.when(at != 0)
    def _():
        bias[...] = rest[pl.ds(share, 1), :]


def finish(core, part, rest):
    rows, width = part.shape
    return pl.pallas_call(
        finish_kernel,
        out_shape=(
            jax.ShapeDtypeStruct((2 * (rows - 8), width), jnp.float32),
            jax.ShapeDtypeStruct((1, width), jnp.float32),
        ),
        in_specs=[whole(SMEM)] + [whole(VMEM)] * 2,
        out_specs=(whole(VMEM),) * 2,
        name="finish",
        compiler_params=pltpu.CompilerParams(vmem_limit_bytes=4 << 20),
    )(core.reshape(1), part, rest)


def shards(features, adj_tiles, tile_index, weight, bias_vec, grad_out):
    core = lax.axis_index("replica")
    row_blocks = 2 * features.shape[0] // adj_tiles.shape[1]
    slots = adj_tiles.shape[0] // 8

    z1 = along_z(features, 1, "z1")
    z2 = along_z(features, 2, "z2")
    r0 = first_hop(features, "r0")
    r0, index = after(r0, tile_index)
    index = lax.all_gather(index, "replica", axis=0, tiled=True)
    pair0 = join(features, r0)
    q0 = second_hop(pair0, "q0")
    other_tiles = swap(adj_tiles, "tiles")
    pair0, again = after(pair0, features)
    z3 = along_z(again, 3, "z3")
    z1, index = after(z1, index)
    pair1 = join(z1, first_hop(z1, "r1"))
    q1 = along_z(q0, 1, "q1")
    z2, other_tiles = after(z2, other_tiles)
    pair2 = join(z2, first_hop(z2, "r2"))
    pair2, other_tiles = after(pair2, other_tiles)
    q2 = second_hop(pair2, "q2")
    z3, pair1, pair2, q0 = after(z3, pair1, pair2, q0)
    pair3 = join(z3, first_hop(z3, "r3"))
    q3 = second_hop(pair3, "q3")
    entries, starts = work_list(index, slots, row_blocks)
    tiles = gather_tiles(entries, starts, adj_tiles, other_tiles)
    work = (entries, starts, tiles)
    acc = add_groups(work, (pair0, q0, pair1), (0, 1, 2), None, row_blocks, "add_a")
    acc = add_groups(work, (q1, pair2), (3, 4), acc, row_blocks, "add_b")
    acc = add_groups(work, (q2, pair3), (5, 6), acc, row_blocks, "add_c")
    mine, give = add_late(work, (q3,), (7,), acc, row_blocks)
    theirs = swap(give, "rows")
    output, keep, give = dense(core, mine, theirs, weight, bias_vec, grad_out)
    part = keep + swap(give, "halves")
    part = part + first_hop(part, "sum1")
    part = part + second_hop(part, "sum2")
    low_part = part.astype(jnp.bfloat16)
    z_parts = [lax.reduce_precision(part, 8, 7)]
    z_parts += [along_z(low_part, k, f"sum{2 + k}").astype(jnp.float32) for k in (1, 2, 3)]
    part = (z_parts[0] + z_parts[1]) + (z_parts[2] + z_parts[3])
    rest = swap(part, "back")
    grad_weight, grad_bias = finish(core, part, rest)
    return output, grad_weight, grad_bias.reshape(bias_vec.shape)


def solution(mesh):
    placed = (
        P(BOTH, None),
        P(BOTH, None, None),
        P(BOTH, None),
        P(),
        P(),
        P(BOTH, None),
    )
    small = mesh.shape["section"] == 16 and mesh.shape["replica"] == 2
    return jax.shard_map(
        shards if small else general_shards,
        mesh=mesh,
        in_specs=placed,
        out_specs=(P(BOTH, None), P(), P()),
        check_vma=False,
    )
```

```python
import functools

import jax
import jax.numpy as jnp
from jax import lax
from jax.experimental import pallas as pl
from jax.experimental.pallas import tpu as pltpu
from jax.sharding import PartitionSpec as P

BOTH = ("section", "replica")
VMEM = pltpu.VMEM
SMEM = pltpu.SMEM


def spread(x, axis, root):
    mine = lax.axis_index(axis) == root
    return lax.psum(jnp.where(mine, x, jnp.zeros_like(x)), axis)


def add_tiles(summed, received, adj_tiles, row_ids, col_ids, first_slot, count, levels):
    tile_part = lax.dynamic_slice_in_dim(adj_tiles, first_slot, count, 0)
    row_pick = lax.dynamic_slice_in_dim(row_ids, first_slot, count, 0)
    col_pick = lax.dynamic_slice_in_dim(col_ids, first_slot, count, 0)
    picked = received[col_pick]
    products = jnp.einsum("kab,kbd->kad", tile_part, picked, preferred_element_type=jnp.float32)
    onehot = (row_pick[:, None] == levels[None, :]).astype(jnp.float32)
    return summed + jnp.einsum("kr,kad->rad", onehot, products, precision=lax.Precision.HIGHEST)


def general_shards(features, adj_tiles, tile_index, weight, bias_vec, grad_out):
    replicas = lax.axis_size("replica")
    replica_idx = lax.axis_index("replica")
    own_slab = lax.all_gather(features, "replica", axis=0, tiled=True)
    rows_slab, feat_width = own_slab.shape
    block_size = adj_tiles.shape[1]
    row_blocks = rows_slab // block_size
    turn_count = lax.axis_size("section") // replicas
    slot_count = adj_tiles.shape[0] // turn_count
    row_ids = tile_index[:, 0]
    col_ids = tile_index[:, 1]
    levels = jnp.arange(row_blocks, dtype=jnp.int32)

    def turn_step(step_idx, summed):
        received = spread(own_slab, "section", replica_idx * turn_count + step_idx)
        received = received.reshape(row_blocks, block_size, feat_width)
        first_slot = step_idx * slot_count
        return add_tiles(
            summed, received, adj_tiles, row_ids, col_ids, first_slot, slot_count, levels
        )

    start_sum = jnp.zeros((row_blocks, block_size, feat_width), jnp.float32)
    partial_sum = lax.fori_loop(0, turn_count, turn_step, start_sum).reshape(rows_slab, feat_width)
    share = rows_slab // replicas
    whole_sum = lax.psum(partial_sum, "replica")
    local_rows = lax.dynamic_slice_in_dim(whole_sum, replica_idx * share, share, 0)
    hidden = local_rows.astype(jnp.bfloat16)
    pre_act = jnp.dot(hidden, weight, preferred_element_type=jnp.float32) + bias_vec
    output = jax.nn.silu(pre_act).astype(jnp.bfloat16)
    sigma = jax.nn.sigmoid(pre_act)
    grad_pre = grad_out.astype(jnp.float32) * sigma * (1.0 + pre_act * (1.0 - sigma))
    grad_low = grad_pre.astype(jnp.bfloat16)
    weight_term = jnp.einsum("nd,ne->de", hidden, grad_low, preferred_element_type=jnp.float32)
    grad_weight, grad_bias = lax.psum((weight_term, jnp.sum(grad_pre, axis=0)), BOTH)
    return (output, grad_weight, grad_bias)


def send(x, target, name):
    perm = [(2 * p + c, 2 * target(p, c) + c) for p in range(16) for c in range(2)]
    with jax.named_scope(name):
        return lax.ppermute(x, BOTH, perm)


def swap(x, name):
    with jax.named_scope(name):
        return lax.ppermute(x, "replica", [(0, 1), (1, 0)])


def first_hop(x, name):
    return send(x, lambda p, c: p ^ (1 if c == 0 else 2), name)


def second_hop(x, name):
    return send(x, lambda p, c: p ^ (2 if c == 0 else 1), name)


def diagonal(x, name):
    return send(x, lambda p, c: p ^ 3, name)


def along_z(x, k, name):
    return send(x, lambda p, c: p ^ (4 * k), name)


def join(own, near):
    return jnp.concatenate([own, near], axis=0)


def after(*arrays):
    return lax.optimization_barrier(arrays)


def narrow(x):
    return x.astype(jnp.bfloat16)


def rounded(x):
    return lax.reduce_precision(x, 8, 7)


def widen(x):
    return x.astype(jnp.float32)


def work_list(index, slots, row_blocks):
    chip = lax.axis_index("section")
    core = lax.axis_index("replica")
    half = row_blocks // 2
    count = index.shape[0] // 2
    tile = jnp.arange(2 * count, dtype=jnp.int32)
    source = tile // slots
    row, col = index[:, 0], index[:, 1]
    live = (row >= 0) & (col // half == core)
    apart = source ^ chip
    x_apart, y_apart, z_apart = apart & 1, (apart >> 1) & 1, apart >> 2
    near = jnp.where(core == 0, x_apart, y_apart)
    far = jnp.where(core == 0, y_apart, x_apart)
    groups = 8
    group = jnp.where(live, 2 * z_apart + far, groups)
    block = half * near + col % half
    mine = tile // count == core
    entry = (tile % count + jnp.where(mine, 0, count)) | (block << 8) | ((row ^ (half * core)) << 12)
    spare = row_blocks << 12
    sizes = jnp.sum((group[:, None] == jnp.arange(groups)[None, :]).astype(jnp.int32), axis=0)
    padded = (sizes + 1) // 2 * 2
    edge = jnp.arange(groups + 1)
    starts = jnp.sum(jnp.where(edge[None, :groups] < edge[:, None], padded[None, :], 0), axis=1)
    same = (group[:, None] == group[None, :]) & (tile[None, :] < tile[:, None])
    rank = jnp.sum(same.astype(jnp.int32), axis=1)
    base = jnp.sum(jnp.where(group[:, None] == edge[None, :groups], starts[None, :groups], 0), axis=1)
    place = jnp.where(live, base + rank, -1)
    length = 2 * count + 2 * groups
    hit = place[None, :] == jnp.arange(length, dtype=jnp.int32)[:, None]
    entries = spare + jnp.sum(jnp.where(hit, (entry - spare)[None, :], 0), axis=1)
    return entries, starts


def gather_kernel(count, entries, starts, own, other, out, sem):
    pairs = starts[8] // 2

    def fetch(m):
        tile = entries[m] & 255

        @pl.when(tile < count)
        def _():
            pltpu.make_async_copy(own.at[tile], out.at[m], sem).start()

        @pl.when(tile >= count)
        def _():
            pltpu.make_async_copy(other.at[tile - count], out.at[m], sem).start()

    def begin(j, carry):
        fetch(2 * j)
        fetch(2 * j + 1)
        return carry

    def finish(size):
        def step(j, carry):
            block = out.at[pl.ds(0, size)]
            pltpu.make_async_copy(own.at[pl.ds(0, size)], block, sem).wait()
            return carry

        return step

    lax.fori_loop(0, pairs, begin, 0)
    lax.fori_loop(0, pairs // 8, finish(16), 0)
    lax.fori_loop(0, pairs % 8, finish(2), 0)


def gather_tiles(entries, starts, own, other):
    size = own.shape[1]
    return pl.pallas_call(
        functools.partial(gather_kernel, own.shape[0]),
        out_shape=VMEM((entries.shape[0], size, size), own.dtype),
        in_specs=[pl.BlockSpec(memory_space=SMEM)] * 2 + [pl.BlockSpec(memory_space=pltpu.HBM)] * 2,
        out_specs=pl.BlockSpec(memory_space=VMEM),
        scratch_shapes=[pltpu.SemaphoreType.DMA],
        name="gather_tiles",
        compiler_params=pltpu.CompilerParams(vmem_limit_bytes=47 << 20),
        cost_estimate=pl.CostEstimate(flops=0, bytes_accessed=1 << 10, transcendentals=0),
    )(entries, starts, own, other)


def add_group(entries, lo, hi, tiles, blocks, acc):
    def product(m):
        at = pl.multiple_of(((entries[m] >> 8) & 15) * 128, 128)
        return jnp.dot(tiles[m], blocks[pl.ds(at, 128), :], preferred_element_type=jnp.float32)

    def add(first, count):
        products = [product(first + i) for i in range(count)]
        for i, p in enumerate(products):
            acc[entries[first + i] >> 12] += p

    def four(j, carry):
        add(lo + 4 * j, 4)
        return carry

    fours = (hi - lo) // 4
    lax.fori_loop(0, fours, four, 0)

    @pl.when((hi - lo) % 4 != 0)
    def _():
        add(lo + 4 * fours, 2)


def add_kernel(groups, fresh, entries, starts, tiles, *refs):
    arrays, acc = refs[: len(groups)], refs[-1]
    if fresh:
        acc[...] = jnp.zeros_like(acc)
    for g, array in zip(groups, arrays):
        add_group(entries, starts[g], starts[g + 1], tiles, array, acc)


def late_kernel(groups, entries, starts, tiles, *refs):
    arrays, (acc, give) = refs[: len(groups)], refs[len(groups) + 1 :]
    for g, array in zip(groups, arrays):
        add_group(entries, starts[g], starts[g + 1], tiles, array, acc)
    half = give.shape[0]
    give[...] = acc[half : 2 * half]


def whole(space):
    return pl.BlockSpec(memory_space=space)


def add_groups(work, arrays, groups, acc, row_blocks, name):
    entries, starts, tiles = work
    shape = VMEM((row_blocks + 1, 128, arrays[0].shape[1]), jnp.float32)
    fresh = acc is None
    return pl.pallas_call(
        functools.partial(add_kernel, groups, fresh),
        out_shape=shape,
        in_specs=[whole(SMEM)] * 2 + [whole(VMEM)] * (1 + len(arrays) + (not fresh)),
        out_specs=whole(VMEM),
        name=name,
        input_output_aliases={} if fresh else {3 + len(arrays): 0},
        compiler_params=pltpu.CompilerParams(vmem_limit_bytes=4 << 20),
        cost_estimate=pl.CostEstimate(flops=16 << 28, bytes_accessed=4 << 20, transcendentals=0),
    )(entries, starts, tiles, *arrays, *([] if fresh else [acc]))


def add_late(work, arrays, groups, acc, row_blocks):
    entries, starts, tiles = work
    half = VMEM((row_blocks // 2, 128, arrays[0].shape[1]), jnp.float32)
    return pl.pallas_call(
        functools.partial(late_kernel, groups),
        out_shape=(VMEM(acc.shape, jnp.float32), half),
        in_specs=[whole(SMEM)] * 2 + [whole(VMEM)] * (2 + len(arrays)),
        out_specs=(whole(VMEM),) * 2,
        name="add_late",
        input_output_aliases={3 + len(arrays): 0},
        compiler_params=pltpu.CompilerParams(vmem_limit_bytes=4 << 20),
        cost_estimate=pl.CostEstimate(flops=1 << 25, bytes_accessed=2 << 20, transcendentals=0),
    )(entries, starts, tiles, *arrays, acc)


def dense_kernel(core, mine, theirs, weight, bias, grad_out, output, keep, give, full):
    hidden = (mine[: theirs.shape[0]] + theirs[...]).reshape(grad_out.shape).astype(jnp.bfloat16)
    pre_act = jnp.dot(hidden, weight[...], preferred_element_type=jnp.float32) + bias[...]
    sigma = 1.0 / (1.0 + jnp.exp(-pre_act))
    output[...] = (pre_act * sigma).astype(jnp.bfloat16)
    grad_pre = grad_out[...].astype(jnp.float32) * sigma * (1.0 + pre_act * (1.0 - sigma))
    grad_low = grad_pre.astype(jnp.bfloat16)
    full[...] = lax.dot_general(
        hidden, grad_low, (((0,), (0,)), ((), ())), preferred_element_type=jnp.float32
    )
    sums = jnp.sum(grad_pre, axis=0, keepdims=True)
    sums = jnp.broadcast_to(sums, (8, sums.shape[1]))
    share = full.shape[0] // 2
    at = core[0]
    keep[:share] = full[pl.ds(pl.multiple_of(at * share, share), share), :]
    give[:share] = full[pl.ds(pl.multiple_of((1 - at) * share, share), share), :]
    keep[share:] = sums
    give[share:] = sums


def dense(core, mine, theirs, weight, bias, grad_out):
    width = weight.shape[0]
    part = VMEM((width // 2 + 8, width), jnp.float32)
    return pl.pallas_call(
        dense_kernel,
        out_shape=(jax.ShapeDtypeStruct(grad_out.shape, jnp.bfloat16), part, part),
        in_specs=[whole(SMEM)] + [whole(VMEM)] * 5,
        out_specs=(whole(VMEM),) * 3,
        scratch_shapes=[VMEM((width, width), jnp.float32)],
        name="dense",
        compiler_params=pltpu.CompilerParams(vmem_limit_bytes=16 << 20),
        cost_estimate=pl.CostEstimate(
            flops=1 << 27, bytes_accessed=2 << 20, transcendentals=1 << 17
        ),
    )(core.reshape(1), mine, theirs, weight, bias.reshape(1, width), grad_out)


def finish_kernel(core, part, rest, weight, bias):
    share = part.shape[0] - 8
    at = core[0]
    weight[pl.ds(pl.multiple_of(at * share, share), share), :] = part[:share]
    weight[pl.ds(pl.multiple_of((1 - at) * share, share), share), :] = rest[:share]

    @pl.when(at == 0)
    def _():
        bias[...] = part[pl.ds(share, 1), :]

    @pl.when(at != 0)
    def _():
        bias[...] = rest[pl.ds(share, 1), :]


def finish(core, part, rest):
    rows, width = part.shape
    return pl.pallas_call(
        finish_kernel,
        out_shape=(
            jax.ShapeDtypeStruct((2 * (rows - 8), width), jnp.float32),
            jax.ShapeDtypeStruct((1, width), jnp.float32),
        ),
        in_specs=[whole(SMEM)] + [whole(VMEM)] * 2,
        out_specs=(whole(VMEM),) * 2,
        name="finish",
        compiler_params=pltpu.CompilerParams(vmem_limit_bytes=4 << 20),
    )(core.reshape(1), part, rest)


def shards(features, adj_tiles, tile_index, weight, bias_vec, grad_out):
    core = lax.axis_index("replica")
    row_blocks = 2 * features.shape[0] // adj_tiles.shape[1]
    slots = adj_tiles.shape[0] // 8

    z1 = along_z(features, 1, "z1")
    z2 = along_z(features, 2, "z2")
    r0 = first_hop(features, "r0")
    r0, index = after(r0, tile_index)
    index = lax.all_gather(index, "replica", axis=0, tiled=True)
    pair0 = join(features, r0)
    q0 = second_hop(pair0, "q0")
    other_tiles = swap(adj_tiles, "tiles")
    pair0, again = after(pair0, features)
    z3 = along_z(again, 3, "z3")
    z1, index = after(z1, index)
    pair1 = join(z1, first_hop(z1, "r1"))
    q1 = along_z(q0, 1, "q1")
    z2, other_tiles = after(z2, other_tiles)
    pair2 = join(z2, first_hop(z2, "r2"))
    pair2, other_tiles = after(pair2, other_tiles)
    q2 = second_hop(pair2, "q2")
    z3, pair1, pair2, q0 = after(z3, pair1, pair2, q0)
    pair3 = join(z3, first_hop(z3, "r3"))
    q3 = second_hop(pair3, "q3")
    entries, starts = work_list(index, slots, row_blocks)
    tiles = gather_tiles(entries, starts, adj_tiles, other_tiles)
    work = (entries, starts, tiles)
    acc = add_groups(work, (pair0, q0, pair1), (0, 1, 2), None, row_blocks, "add_a")
    acc = add_groups(work, (q1, pair2), (3, 4), acc, row_blocks, "add_b")
    acc = add_groups(work, (q2, pair3), (5, 6), acc, row_blocks, "add_c")
    mine, give = add_late(work, (q3,), (7,), acc, row_blocks)
    theirs = swap(give, "rows")
    output, keep, give = dense(core, mine, theirs, weight, bias_vec, grad_out)
    part = keep + swap(give, "halves")
    low = narrow(part)
    near = widen(first_hop(low, "sum1"))
    far = widen(second_hop(low, "sum2"))
    across = widen(diagonal(low, "sumd"))
    part = (rounded(part) + across) + (near + far)
    low_part = part.astype(jnp.bfloat16)
    z_parts = [lax.reduce_precision(part, 8, 7)]
    z_parts += [along_z(low_part, k, f"sum{2 + k}").astype(jnp.float32) for k in (3, 2, 1)]
    part = (z_parts[0] + z_parts[3]) + (z_parts[2] + z_parts[1])
    rest = swap(part, "back")
    grad_weight, grad_bias = finish(core, part, rest)
    return output, grad_weight, grad_bias.reshape(bias_vec.shape)


def solution(mesh):
    placed = (
        P(BOTH, None),
        P(BOTH, None, None),
        P(BOTH, None),
        P(),
        P(),
        P(BOTH, None),
    )
    small = mesh.shape["section"] == 16 and mesh.shape["replica"] == 2
    return jax.shard_map(
        shards if small else general_shards,
        mesh=mesh,
        in_specs=placed,
        out_specs=(P(BOTH, None), P(), P()),
        check_vma=False,
    )
```

```python
import functools

import jax
import jax.numpy as jnp
from jax import lax
from jax.experimental import pallas as pl
from jax.experimental.pallas import tpu as pltpu
from jax.sharding import PartitionSpec as P

BOTH = ("section", "replica")
VMEM = pltpu.VMEM
SMEM = pltpu.SMEM


def spread(x, axis, root):
    mine = lax.axis_index(axis) == root
    return lax.psum(jnp.where(mine, x, jnp.zeros_like(x)), axis)


def add_tiles(summed, received, adj_tiles, row_ids, col_ids, first_slot, count, levels):
    tile_part = lax.dynamic_slice_in_dim(adj_tiles, first_slot, count, 0)
    row_pick = lax.dynamic_slice_in_dim(row_ids, first_slot, count, 0)
    col_pick = lax.dynamic_slice_in_dim(col_ids, first_slot, count, 0)
    picked = received[col_pick]
    products = jnp.einsum("kab,kbd->kad", tile_part, picked, preferred_element_type=jnp.float32)
    onehot = (row_pick[:, None] == levels[None, :]).astype(jnp.float32)
    return summed + jnp.einsum("kr,kad->rad", onehot, products, precision=lax.Precision.HIGHEST)


def general_shards(features, adj_tiles, tile_index, weight, bias_vec, grad_out):
    replicas = lax.axis_size("replica")
    replica_idx = lax.axis_index("replica")
    own_slab = lax.all_gather(features, "replica", axis=0, tiled=True)
    rows_slab, feat_width = own_slab.shape
    block_size = adj_tiles.shape[1]
    row_blocks = rows_slab // block_size
    turn_count = lax.axis_size("section") // replicas
    slot_count = adj_tiles.shape[0] // turn_count
    row_ids = tile_index[:, 0]
    col_ids = tile_index[:, 1]
    levels = jnp.arange(row_blocks, dtype=jnp.int32)

    def turn_step(step_idx, summed):
        received = spread(own_slab, "section", replica_idx * turn_count + step_idx)
        received = received.reshape(row_blocks, block_size, feat_width)
        first_slot = step_idx * slot_count
        return add_tiles(
            summed, received, adj_tiles, row_ids, col_ids, first_slot, slot_count, levels
        )

    start_sum = jnp.zeros((row_blocks, block_size, feat_width), jnp.float32)
    partial_sum = lax.fori_loop(0, turn_count, turn_step, start_sum).reshape(rows_slab, feat_width)
    share = rows_slab // replicas
    whole_sum = lax.psum(partial_sum, "replica")
    local_rows = lax.dynamic_slice_in_dim(whole_sum, replica_idx * share, share, 0)
    hidden = local_rows.astype(jnp.bfloat16)
    pre_act = jnp.dot(hidden, weight, preferred_element_type=jnp.float32) + bias_vec
    output = jax.nn.silu(pre_act).astype(jnp.bfloat16)
    sigma = jax.nn.sigmoid(pre_act)
    grad_pre = grad_out.astype(jnp.float32) * sigma * (1.0 + pre_act * (1.0 - sigma))
    grad_low = grad_pre.astype(jnp.bfloat16)
    weight_term = jnp.einsum("nd,ne->de", hidden, grad_low, preferred_element_type=jnp.float32)
    grad_weight, grad_bias = lax.psum((weight_term, jnp.sum(grad_pre, axis=0)), BOTH)
    return (output, grad_weight, grad_bias)


def send(x, target, name):
    perm = [(2 * p + c, 2 * target(p, c) + c) for p in range(16) for c in range(2)]
    with jax.named_scope(name):
        return lax.ppermute(x, BOTH, perm)


def swap(x, name):
    with jax.named_scope(name):
        return lax.ppermute(x, "replica", [(0, 1), (1, 0)])


def first_hop(x, name):
    return send(x, lambda p, c: p ^ (1 if c == 0 else 2), name)


def second_hop(x, name):
    return send(x, lambda p, c: p ^ (2 if c == 0 else 1), name)


def diagonal(x, name):
    return send(x, lambda p, c: p ^ 3, name)


def along_z(x, k, name):
    return send(x, lambda p, c: p ^ (4 * k), name)


def join(own, near):
    return jnp.concatenate([own, near], axis=0)


def after(*arrays):
    return lax.optimization_barrier(arrays)


def narrow(x):
    return x.astype(jnp.bfloat16)


def rounded(x):
    return lax.reduce_precision(x, 8, 7)


def widen(x):
    return x.astype(jnp.float32)


def work_list(index, slots, row_blocks):
    chip = lax.axis_index("section")
    core = lax.axis_index("replica")
    half = row_blocks // 2
    count = index.shape[0] // 2
    tile = jnp.arange(2 * count, dtype=jnp.int32)
    source = tile // slots
    row, col = index[:, 0], index[:, 1]
    live = (row >= 0) & (col // half == core)
    apart = source ^ chip
    x_apart, y_apart, z_apart = apart & 1, (apart >> 1) & 1, apart >> 2
    near = jnp.where(core == 0, x_apart, y_apart)
    far = jnp.where(core == 0, y_apart, x_apart)
    groups = 8
    group = jnp.where(live, 2 * z_apart + far, groups)
    block = half * near + col % half
    mine = tile // count == core
    entry = (tile % count + jnp.where(mine, 0, count)) | (block << 8) | ((row ^ (half * core)) << 12)
    spare = row_blocks << 12
    sizes = jnp.sum((group[:, None] == jnp.arange(groups)[None, :]).astype(jnp.int32), axis=0)
    padded = (sizes + 1) // 2 * 2
    edge = jnp.arange(groups + 1)
    starts = jnp.sum(jnp.where(edge[None, :groups] < edge[:, None], padded[None, :], 0), axis=1)
    same = (group[:, None] == group[None, :]) & (tile[None, :] < tile[:, None])
    rank = jnp.sum(same.astype(jnp.int32), axis=1)
    base = jnp.sum(jnp.where(group[:, None] == edge[None, :groups], starts[None, :groups], 0), axis=1)
    place = jnp.where(live, base + rank, -1)
    length = 2 * count + 2 * groups
    hit = place[None, :] == jnp.arange(length, dtype=jnp.int32)[:, None]
    entries = spare + jnp.sum(jnp.where(hit, (entry - spare)[None, :], 0), axis=1)
    return entries, starts


def gather_kernel(count, entries, starts, own, other, out, sem):
    pairs = starts[8] // 2

    def fetch(m):
        tile = entries[m] & 255

        @pl.when(tile < count)
        def _():
            pltpu.make_async_copy(own.at[tile], out.at[m], sem).start()

        @pl.when(tile >= count)
        def _():
            pltpu.make_async_copy(other.at[tile - count], out.at[m], sem).start()

    def begin(j, carry):
        fetch(2 * j)
        fetch(2 * j + 1)
        return carry

    def finish(size):
        def step(j, carry):
            block = out.at[pl.ds(0, size)]
            pltpu.make_async_copy(own.at[pl.ds(0, size)], block, sem).wait()
            return carry

        return step

    lax.fori_loop(0, pairs, begin, 0)
    lax.fori_loop(0, pairs // 8, finish(16), 0)
    lax.fori_loop(0, pairs % 8, finish(2), 0)


def gather_tiles(entries, starts, own, other):
    size = own.shape[1]
    return pl.pallas_call(
        functools.partial(gather_kernel, own.shape[0]),
        out_shape=VMEM((entries.shape[0], size, size), own.dtype),
        in_specs=[pl.BlockSpec(memory_space=SMEM)] * 2 + [pl.BlockSpec(memory_space=pltpu.HBM)] * 2,
        out_specs=pl.BlockSpec(memory_space=VMEM),
        scratch_shapes=[pltpu.SemaphoreType.DMA],
        name="gather_tiles",
        compiler_params=pltpu.CompilerParams(vmem_limit_bytes=47 << 20),
        cost_estimate=pl.CostEstimate(flops=0, bytes_accessed=1 << 10, transcendentals=0),
    )(entries, starts, own, other)


def add_group(entries, lo, hi, tiles, blocks, acc):
    def product(m):
        at = pl.multiple_of(((entries[m] >> 8) & 15) * 128, 128)
        return jnp.dot(tiles[m], blocks[pl.ds(at, 128), :], preferred_element_type=jnp.float32)

    def add(first, count):
        products = [product(first + i) for i in range(count)]
        for i, p in enumerate(products):
            acc[entries[first + i] >> 12] += p

    def four(j, carry):
        add(lo + 4 * j, 4)
        return carry

    fours = (hi - lo) // 4
    lax.fori_loop(0, fours, four, 0)

    @pl.when((hi - lo) % 4 != 0)
    def _():
        add(lo + 4 * fours, 2)


def add_kernel(groups, fresh, entries, starts, tiles, *refs):
    arrays, acc = refs[: len(groups)], refs[-1]
    if fresh:
        acc[...] = jnp.zeros_like(acc)
    for g, array in zip(groups, arrays):
        add_group(entries, starts[g], starts[g + 1], tiles, array, acc)


def late_kernel(groups, entries, starts, tiles, *refs):
    arrays, (acc, give) = refs[: len(groups)], refs[len(groups) + 1 :]
    for g, array in zip(groups, arrays):
        add_group(entries, starts[g], starts[g + 1], tiles, array, acc)
    half = give.shape[0]
    give[...] = acc[half : 2 * half].astype(give.dtype)


def whole(space):
    return pl.BlockSpec(memory_space=space)


def add_groups(work, arrays, groups, acc, row_blocks, name):
    entries, starts, tiles = work
    shape = VMEM((row_blocks + 1, 128, arrays[0].shape[1]), jnp.float32)
    fresh = acc is None
    return pl.pallas_call(
        functools.partial(add_kernel, groups, fresh),
        out_shape=shape,
        in_specs=[whole(SMEM)] * 2 + [whole(VMEM)] * (1 + len(arrays) + (not fresh)),
        out_specs=whole(VMEM),
        name=name,
        input_output_aliases={} if fresh else {3 + len(arrays): 0},
        compiler_params=pltpu.CompilerParams(vmem_limit_bytes=4 << 20),
        cost_estimate=pl.CostEstimate(flops=16 << 28, bytes_accessed=4 << 20, transcendentals=0),
    )(entries, starts, tiles, *arrays, *([] if fresh else [acc]))


def add_late(work, arrays, groups, acc, row_blocks):
    entries, starts, tiles = work
    half = VMEM((row_blocks // 2, 128, arrays[0].shape[1]), jnp.bfloat16)
    return pl.pallas_call(
        functools.partial(late_kernel, groups),
        out_shape=(VMEM(acc.shape, jnp.float32), half),
        in_specs=[whole(SMEM)] * 2 + [whole(VMEM)] * (2 + len(arrays)),
        out_specs=(whole(VMEM),) * 2,
        name="add_late",
        input_output_aliases={3 + len(arrays): 0},
        compiler_params=pltpu.CompilerParams(vmem_limit_bytes=4 << 20),
        cost_estimate=pl.CostEstimate(flops=1 << 25, bytes_accessed=2 << 20, transcendentals=0),
    )(entries, starts, tiles, *arrays, acc)


def dense_kernel(core, mine, theirs, weight, bias, grad_out, output, keep, give, full):
    hidden = (mine[: theirs.shape[0]] + theirs[...].astype(jnp.float32)).reshape(grad_out.shape).astype(jnp.bfloat16)
    pre_act = jnp.dot(hidden, weight[...], preferred_element_type=jnp.float32) + bias[...]
    sigma = 1.0 / (1.0 + jnp.exp(-pre_act))
    output[...] = (pre_act * sigma).astype(jnp.bfloat16)
    grad_pre = grad_out[...].astype(jnp.float32) * sigma * (1.0 + pre_act * (1.0 - sigma))
    grad_low = grad_pre.astype(jnp.bfloat16)
    full[...] = lax.dot_general(
        hidden, grad_low, (((0,), (0,)), ((), ())), preferred_element_type=jnp.float32
    )
    sums = jnp.sum(grad_pre, axis=0, keepdims=True)
    sums = jnp.broadcast_to(sums, (8, sums.shape[1]))
    share = full.shape[0] // 2
    at = core[0]
    keep[:share] = full[pl.ds(pl.multiple_of(at * share, share), share), :]
    give[:share] = full[pl.ds(pl.multiple_of((1 - at) * share, share), share), :]
    keep[share:] = sums
    give[share:] = sums


def dense(core, mine, theirs, weight, bias, grad_out):
    width = weight.shape[0]
    part = VMEM((width // 2 + 8, width), jnp.float32)
    return pl.pallas_call(
        dense_kernel,
        out_shape=(jax.ShapeDtypeStruct(grad_out.shape, jnp.bfloat16), part, part),
        in_specs=[whole(SMEM)] + [whole(VMEM)] * 5,
        out_specs=(whole(VMEM),) * 3,
        scratch_shapes=[VMEM((width, width), jnp.float32)],
        name="dense",
        compiler_params=pltpu.CompilerParams(vmem_limit_bytes=16 << 20),
        cost_estimate=pl.CostEstimate(
            flops=1 << 27, bytes_accessed=2 << 20, transcendentals=1 << 17
        ),
    )(core.reshape(1), mine, theirs, weight, bias.reshape(1, width), grad_out)


def finish_kernel(core, part, rest, weight, bias):
    share = part.shape[0] - 8
    at = core[0]
    weight[pl.ds(pl.multiple_of(at * share, share), share), :] = part[:share]
    weight[pl.ds(pl.multiple_of((1 - at) * share, share), share), :] = rest[:share]

    @pl.when(at == 0)
    def _():
        bias[...] = part[pl.ds(share, 1), :]

    @pl.when(at != 0)
    def _():
        bias[...] = rest[pl.ds(share, 1), :]


def finish(core, part, rest):
    rows, width = part.shape
    return pl.pallas_call(
        finish_kernel,
        out_shape=(
            jax.ShapeDtypeStruct((2 * (rows - 8), width), jnp.float32),
            jax.ShapeDtypeStruct((1, width), jnp.float32),
        ),
        in_specs=[whole(SMEM)] + [whole(VMEM)] * 2,
        out_specs=(whole(VMEM),) * 2,
        name="finish",
        compiler_params=pltpu.CompilerParams(vmem_limit_bytes=4 << 20),
    )(core.reshape(1), part, rest)


def shards(features, adj_tiles, tile_index, weight, bias_vec, grad_out):
    core = lax.axis_index("replica")
    row_blocks = 2 * features.shape[0] // adj_tiles.shape[1]
    slots = adj_tiles.shape[0] // 8

    z1 = along_z(features, 1, "z1")
    z2 = along_z(features, 2, "z2")
    r0 = first_hop(features, "r0")
    r0, index = after(r0, tile_index)
    index = lax.all_gather(index, "replica", axis=0, tiled=True)
    pair0 = join(features, r0)
    q0 = second_hop(pair0, "q0")
    other_tiles = swap(adj_tiles, "tiles")
    pair0, again = after(pair0, features)
    z3 = along_z(again, 3, "z3")
    z1, index = after(z1, index)
    pair1 = join(z1, first_hop(z1, "r1"))
    q1 = along_z(q0, 1, "q1")
    z2, other_tiles = after(z2, other_tiles)
    r2 = first_hop(z2, "r2")
    q2a = second_hop(z2, "q2a")
    pair2 = join(z2, r2)
    q2a, other_tiles = after(q2a, other_tiles)
    q2 = join(q2a, second_hop(r2, "q2b"))
    z3, pair1, pair2, q0 = after(z3, pair1, pair2, q0)
    r3 = first_hop(z3, "r3")
    q3a = second_hop(z3, "q3a")
    pair3 = join(z3, r3)
    q1, pair3 = after(q1, pair3)
    q3 = join(q3a, second_hop(r3, "q3b"))
    entries, starts = work_list(index, slots, row_blocks)
    tiles = gather_tiles(entries, starts, adj_tiles, other_tiles)
    work = (entries, starts, tiles)
    acc = add_groups(work, (pair0, q0, pair1), (0, 1, 2), None, row_blocks, "add_a")
    acc = add_groups(work, (q1, pair2), (3, 4), acc, row_blocks, "add_b")
    acc = add_groups(work, (q2, pair3), (5, 6), acc, row_blocks, "add_c")
    mine, give = add_late(work, (q3,), (7,), acc, row_blocks)
    theirs = swap(give, "rows")
    output, keep, give = dense(core, mine, theirs, weight, bias_vec, grad_out)
    part = keep + swap(give, "halves")
    low = narrow(part)
    near = widen(first_hop(low, "sum1"))
    far = widen(second_hop(low, "sum2"))
    across = widen(diagonal(low, "sumd"))
    part = (rounded(part) + across) + (near + far)
    low_part = part.astype(jnp.bfloat16)
    z_parts = [lax.reduce_precision(part, 8, 7)]
    z_parts += [along_z(low_part, k, f"sum{2 + k}").astype(jnp.float32) for k in (3, 2, 1)]
    part = (z_parts[0] + z_parts[3]) + (z_parts[2] + z_parts[1])
    rest = swap(part, "back")
    grad_weight, grad_bias = finish(core, part, rest)
    return output, grad_weight, grad_bias.reshape(bias_vec.shape)


def solution(mesh):
    placed = (
        P(BOTH, None),
        P(BOTH, None, None),
        P(BOTH, None),
        P(),
        P(),
        P(BOTH, None),
    )
    small = mesh.shape["section"] == 16 and mesh.shape["replica"] == 2
    return jax.shard_map(
        shards if small else general_shards,
        mesh=mesh,
        in_specs=placed,
        out_specs=(P(BOTH, None), P(), P()),
        check_vma=False,
    )
```

```python
import functools

import jax
import jax.numpy as jnp
from jax import lax
from jax.experimental import pallas as pl
from jax.experimental.pallas import tpu as pltpu
from jax.sharding import PartitionSpec as P

BOTH = ("section", "replica")
VMEM = pltpu.VMEM
SMEM = pltpu.SMEM


def spread(x, axis, root):
    mine = lax.axis_index(axis) == root
    return lax.psum(jnp.where(mine, x, jnp.zeros_like(x)), axis)


def add_tiles(summed, received, adj_tiles, row_ids, col_ids, first_slot, count, levels):
    tile_part = lax.dynamic_slice_in_dim(adj_tiles, first_slot, count, 0)
    row_pick = lax.dynamic_slice_in_dim(row_ids, first_slot, count, 0)
    col_pick = lax.dynamic_slice_in_dim(col_ids, first_slot, count, 0)
    picked = received[col_pick]
    products = jnp.einsum("kab,kbd->kad", tile_part, picked, preferred_element_type=jnp.float32)
    onehot = (row_pick[:, None] == levels[None, :]).astype(jnp.float32)
    return summed + jnp.einsum("kr,kad->rad", onehot, products, precision=lax.Precision.HIGHEST)


def general_shards(features, adj_tiles, tile_index, weight, bias_vec, grad_out):
    replicas = lax.axis_size("replica")
    replica_idx = lax.axis_index("replica")
    own_slab = lax.all_gather(features, "replica", axis=0, tiled=True)
    rows_slab, feat_width = own_slab.shape
    block_size = adj_tiles.shape[1]
    row_blocks = rows_slab // block_size
    turn_count = lax.axis_size("section") // replicas
    slot_count = adj_tiles.shape[0] // turn_count
    row_ids = tile_index[:, 0]
    col_ids = tile_index[:, 1]
    levels = jnp.arange(row_blocks, dtype=jnp.int32)

    def turn_step(step_idx, summed):
        received = spread(own_slab, "section", replica_idx * turn_count + step_idx)
        received = received.reshape(row_blocks, block_size, feat_width)
        first_slot = step_idx * slot_count
        return add_tiles(
            summed, received, adj_tiles, row_ids, col_ids, first_slot, slot_count, levels
        )

    start_sum = jnp.zeros((row_blocks, block_size, feat_width), jnp.float32)
    partial_sum = lax.fori_loop(0, turn_count, turn_step, start_sum).reshape(rows_slab, feat_width)
    share = rows_slab // replicas
    whole_sum = lax.psum(partial_sum, "replica")
    local_rows = lax.dynamic_slice_in_dim(whole_sum, replica_idx * share, share, 0)
    hidden = local_rows.astype(jnp.bfloat16)
    pre_act = jnp.dot(hidden, weight, preferred_element_type=jnp.float32) + bias_vec
    output = jax.nn.silu(pre_act).astype(jnp.bfloat16)
    sigma = jax.nn.sigmoid(pre_act)
    grad_pre = grad_out.astype(jnp.float32) * sigma * (1.0 + pre_act * (1.0 - sigma))
    grad_low = grad_pre.astype(jnp.bfloat16)
    weight_term = jnp.einsum("nd,ne->de", hidden, grad_low, preferred_element_type=jnp.float32)
    grad_weight, grad_bias = lax.psum((weight_term, jnp.sum(grad_pre, axis=0)), BOTH)
    return (output, grad_weight, grad_bias)


def send(x, target, name):
    perm = [(2 * p + c, 2 * target(p, c) + c) for p in range(16) for c in range(2)]
    with jax.named_scope(name):
        return lax.ppermute(x, BOTH, perm)


def swap(x, name):
    with jax.named_scope(name):
        return lax.ppermute(x, "replica", [(0, 1), (1, 0)])


def first_hop(x, name):
    return send(x, lambda p, c: p ^ (1 if c == 0 else 2), name)


def second_hop(x, name):
    return send(x, lambda p, c: p ^ (2 if c == 0 else 1), name)


def diagonal(x, name):
    return send(x, lambda p, c: p ^ 3, name)


def along_z(x, k, name):
    return send(x, lambda p, c: p ^ (4 * k), name)


def join(own, near):
    return jnp.concatenate([own, near], axis=0)


def after(*arrays):
    return lax.optimization_barrier(arrays)


def narrow(x):
    return x.astype(jnp.bfloat16)


def rounded(x):
    return lax.reduce_precision(x, 8, 7)


def widen(x):
    return x.astype(jnp.float32)


def work_list(index, slots, row_blocks):
    chip = lax.axis_index("section")
    core = lax.axis_index("replica")
    half = row_blocks // 2
    count = index.shape[0] // 2
    tile = jnp.arange(2 * count, dtype=jnp.int32)
    source = tile // slots
    row, col = index[:, 0], index[:, 1]
    live = (row >= 0) & (col // half == core)
    apart = source ^ chip
    x_apart, y_apart, z_apart = apart & 1, (apart >> 1) & 1, apart >> 2
    near = jnp.where(core == 0, x_apart, y_apart)
    far = jnp.where(core == 0, y_apart, x_apart)
    groups = 8
    group = jnp.where(live, 2 * z_apart + far, groups)
    block = half * near + col % half
    mine = tile // count == core
    entry = (tile % count + jnp.where(mine, 0, count)) | (block << 8) | ((row ^ (half * core)) << 12)
    spare = row_blocks << 12
    sizes = jnp.sum((group[:, None] == jnp.arange(groups)[None, :]).astype(jnp.int32), axis=0)
    padded = (sizes + 1) // 2 * 2
    edge = jnp.arange(groups + 1)
    starts = jnp.sum(jnp.where(edge[None, :groups] < edge[:, None], padded[None, :], 0), axis=1)
    same = (group[:, None] == group[None, :]) & (tile[None, :] < tile[:, None])
    rank = jnp.sum(same.astype(jnp.int32), axis=1)
    base = jnp.sum(jnp.where(group[:, None] == edge[None, :groups], starts[None, :groups], 0), axis=1)
    place = jnp.where(live, base + rank, -1)
    length = 2 * count + 2 * groups
    hit = place[None, :] == jnp.arange(length, dtype=jnp.int32)[:, None]
    entries = spare + jnp.sum(jnp.where(hit, (entry - spare)[None, :], 0), axis=1)
    return entries, starts


def gather_kernel(count, entries, starts, own, other, out, sem):
    pairs = starts[8] // 2

    def fetch(m):
        tile = entries[m] & 255

        @pl.when(tile < count)
        def _():
            pltpu.make_async_copy(own.at[tile], out.at[m], sem).start()

        @pl.when(tile >= count)
        def _():
            pltpu.make_async_copy(other.at[tile - count], out.at[m], sem).start()

    def begin(j, carry):
        fetch(2 * j)
        fetch(2 * j + 1)
        return carry

    def finish(size):
        def step(j, carry):
            block = out.at[pl.ds(0, size)]
            pltpu.make_async_copy(own.at[pl.ds(0, size)], block, sem).wait()
            return carry

        return step

    lax.fori_loop(0, pairs, begin, 0)
    lax.fori_loop(0, pairs // 8, finish(16), 0)
    lax.fori_loop(0, pairs % 8, finish(2), 0)


def gather_tiles(entries, starts, own, other):
    size = own.shape[1]
    return pl.pallas_call(
        functools.partial(gather_kernel, own.shape[0]),
        out_shape=VMEM((entries.shape[0], size, size), own.dtype),
        in_specs=[pl.BlockSpec(memory_space=SMEM)] * 2 + [pl.BlockSpec(memory_space=pltpu.HBM)] * 2,
        out_specs=pl.BlockSpec(memory_space=VMEM),
        scratch_shapes=[pltpu.SemaphoreType.DMA],
        name="gather_tiles",
        compiler_params=pltpu.CompilerParams(vmem_limit_bytes=47 << 20),
        cost_estimate=pl.CostEstimate(flops=0, bytes_accessed=1 << 10, transcendentals=0),
    )(entries, starts, own, other)


def add_group(entries, lo, hi, tiles, blocks, acc):
    def product(m):
        at = pl.multiple_of(((entries[m] >> 8) & 15) * 128, 128)
        return jnp.dot(tiles[m], blocks[pl.ds(at, 128), :], preferred_element_type=jnp.float32)

    def add(first, count):
        products = [product(first + i) for i in range(count)]
        for i, p in enumerate(products):
            acc[entries[first + i] >> 12] += p

    def four(j, carry):
        add(lo + 4 * j, 4)
        return carry

    fours = (hi - lo) // 4
    lax.fori_loop(0, fours, four, 0)

    @pl.when((hi - lo) % 4 != 0)
    def _():
        add(lo + 4 * fours, 2)


def add_kernel(groups, fresh, entries, starts, tiles, *refs):
    arrays, acc = refs[: len(groups)], refs[-1]
    if fresh:
        acc[...] = jnp.zeros_like(acc)
    for g, array in zip(groups, arrays):
        add_group(entries, starts[g], starts[g + 1], tiles, array, acc)


def late_kernel(groups, entries, starts, tiles, *refs):
    arrays, (acc, give) = refs[: len(groups)], refs[len(groups) + 1 :]
    for g, array in zip(groups, arrays):
        add_group(entries, starts[g], starts[g + 1], tiles, array, acc)
    half = give.shape[0]
    give[...] = acc[half : 2 * half]


def whole(space):
    return pl.BlockSpec(memory_space=space)


def add_groups(work, arrays, groups, acc, row_blocks, name):
    entries, starts, tiles = work
    shape = VMEM((row_blocks + 1, 128, arrays[0].shape[1]), jnp.float32)
    fresh = acc is None
    return pl.pallas_call(
        functools.partial(add_kernel, groups, fresh),
        out_shape=shape,
        in_specs=[whole(SMEM)] * 2 + [whole(VMEM)] * (1 + len(arrays) + (not fresh)),
        out_specs=whole(VMEM),
        name=name,
        input_output_aliases={} if fresh else {3 + len(arrays): 0},
        compiler_params=pltpu.CompilerParams(vmem_limit_bytes=4 << 20),
        cost_estimate=pl.CostEstimate(flops=16 << 28, bytes_accessed=4 << 20, transcendentals=0),
    )(entries, starts, tiles, *arrays, *([] if fresh else [acc]))


def add_late(work, arrays, groups, acc, row_blocks):
    entries, starts, tiles = work
    half = VMEM((row_blocks // 2, 128, arrays[0].shape[1]), jnp.float32)
    return pl.pallas_call(
        functools.partial(late_kernel, groups),
        out_shape=(VMEM(acc.shape, jnp.float32), half),
        in_specs=[whole(SMEM)] * 2 + [whole(VMEM)] * (2 + len(arrays)),
        out_specs=(whole(VMEM),) * 2,
        name="add_late",
        input_output_aliases={3 + len(arrays): 0},
        compiler_params=pltpu.CompilerParams(vmem_limit_bytes=4 << 20),
        cost_estimate=pl.CostEstimate(flops=1 << 25, bytes_accessed=2 << 20, transcendentals=0),
    )(entries, starts, tiles, *arrays, acc)


def dense_kernel(core, mine, theirs, weight, bias, grad_out, output, keep, give, full):
    hidden = (mine[: theirs.shape[0]] + theirs[...]).reshape(grad_out.shape).astype(jnp.bfloat16)
    pre_act = jnp.dot(hidden, weight[...], preferred_element_type=jnp.float32) + bias[...]
    sigma = 1.0 / (1.0 + jnp.exp(-pre_act))
    output[...] = (pre_act * sigma).astype(jnp.bfloat16)
    grad_pre = grad_out[...].astype(jnp.float32) * sigma * (1.0 + pre_act * (1.0 - sigma))
    grad_low = grad_pre.astype(jnp.bfloat16)
    full[...] = lax.dot_general(
        hidden, grad_low, (((0,), (0,)), ((), ())), preferred_element_type=jnp.float32
    )
    sums = jnp.sum(grad_pre, axis=0, keepdims=True)
    sums = jnp.broadcast_to(sums, (8, sums.shape[1]))
    share = full.shape[0] // 2
    at = core[0]
    keep[:share] = full[pl.ds(pl.multiple_of(at * share, share), share), :]
    give[:share] = full[pl.ds(pl.multiple_of((1 - at) * share, share), share), :]
    keep[share:] = sums
    give[share:] = sums


def dense(core, mine, theirs, weight, bias, grad_out):
    width = weight.shape[0]
    part = VMEM((width // 2 + 8, width), jnp.float32)
    return pl.pallas_call(
        dense_kernel,
        out_shape=(jax.ShapeDtypeStruct(grad_out.shape, jnp.bfloat16), part, part),
        in_specs=[whole(SMEM)] + [whole(VMEM)] * 5,
        out_specs=(whole(VMEM),) * 3,
        scratch_shapes=[VMEM((width, width), jnp.float32)],
        name="dense",
        compiler_params=pltpu.CompilerParams(vmem_limit_bytes=16 << 20),
        cost_estimate=pl.CostEstimate(
            flops=1 << 27, bytes_accessed=2 << 20, transcendentals=1 << 17
        ),
    )(core.reshape(1), mine, theirs, weight, bias.reshape(1, width), grad_out)


def finish_kernel(core, part, rest, weight, bias):
    share = part.shape[0] - 8
    at = core[0]
    weight[pl.ds(pl.multiple_of(at * share, share), share), :] = part[:share]
    weight[pl.ds(pl.multiple_of((1 - at) * share, share), share), :] = rest[:share]

    @pl.when(at == 0)
    def _():
        bias[...] = part[pl.ds(share, 1), :]

    @pl.when(at != 0)
    def _():
        bias[...] = rest[pl.ds(share, 1), :]


def finish(core, part, rest):
    rows, width = part.shape
    return pl.pallas_call(
        finish_kernel,
        out_shape=(
            jax.ShapeDtypeStruct((2 * (rows - 8), width), jnp.float32),
            jax.ShapeDtypeStruct((1, width), jnp.float32),
        ),
        in_specs=[whole(SMEM)] + [whole(VMEM)] * 2,
        out_specs=(whole(VMEM),) * 2,
        name="finish",
        compiler_params=pltpu.CompilerParams(vmem_limit_bytes=4 << 20),
    )(core.reshape(1), part, rest)


def shards(features, adj_tiles, tile_index, weight, bias_vec, grad_out):
    core = lax.axis_index("replica")
    row_blocks = 2 * features.shape[0] // adj_tiles.shape[1]
    slots = adj_tiles.shape[0] // 8

    z1 = along_z(features, 1, "z1")
    z2 = along_z(features, 2, "z2")
    r0 = first_hop(features, "r0")
    r0, index = after(r0, tile_index)
    index = lax.all_gather(index, "replica", axis=0, tiled=True)
    pair0 = join(features, r0)
    q0 = second_hop(pair0, "q0")
    other_tiles = swap(adj_tiles, "tiles")
    pair0, again = after(pair0, features)
    z3 = along_z(again, 3, "z3")
    z1, index = after(z1, index)
    pair1 = join(z1, first_hop(z1, "r1"))
    q1 = along_z(q0, 1, "q1")
    z2, other_tiles = after(z2, other_tiles)
    r2 = first_hop(z2, "r2")
    q2a = second_hop(z2, "q2a")
    pair2 = join(z2, r2)
    q2a, other_tiles = after(q2a, other_tiles)
    q2 = join(q2a, second_hop(r2, "q2b"))
    z3, pair1, pair2, q0 = after(z3, pair1, pair2, q0)
    r3 = first_hop(z3, "r3")
    q3a = second_hop(z3, "q3a")
    pair3 = join(z3, r3)
    q1, pair3 = after(q1, pair3)
    q3 = join(q3a, second_hop(r3, "q3b"))
    entries, starts = work_list(index, slots, row_blocks)
    tiles = gather_tiles(entries, starts, adj_tiles, other_tiles)
    work = (entries, starts, tiles)
    acc = add_groups(work, (pair0, q0, pair1), (0, 1, 2), None, row_blocks, "add_a")
    acc = add_groups(work, (q1, pair2), (3, 4), acc, row_blocks, "add_b")
    acc = add_groups(work, (q2, pair3), (5, 6), acc, row_blocks, "add_c")
    mine, give = add_late(work, (q3,), (7,), acc, row_blocks)
    theirs = swap(give, "rows")
    output, keep, give = dense(core, mine, theirs, weight, bias_vec, grad_out)
    part = keep + swap(give, "halves")
    low = narrow(part)
    near = widen(first_hop(low, "sum1"))
    far = widen(second_hop(low, "sum2"))
    across = widen(diagonal(low, "sumd"))
    part = (rounded(part) + across) + (near + far)
    low_part = part.astype(jnp.bfloat16)
    z_parts = [lax.reduce_precision(part, 8, 7)]
    z_parts += [along_z(low_part, k, f"sum{2 + k}").astype(jnp.float32) for k in (3, 2, 1)]
    part = (z_parts[0] + z_parts[3]) + (z_parts[2] + z_parts[1])
    rest = swap(part, "back")
    grad_weight, grad_bias = finish(core, part, rest)
    return output, grad_weight, grad_bias.reshape(bias_vec.shape)


def solution(mesh):
    placed = (
        P(BOTH, None),
        P(BOTH, None, None),
        P(BOTH, None),
        P(),
        P(),
        P(BOTH, None),
    )
    small = mesh.shape["section"] == 16 and mesh.shape["replica"] == 2
    return jax.shard_map(
        shards if small else general_shards,
        mesh=mesh,
        in_specs=placed,
        out_specs=(P(BOTH, None), P(), P()),
        check_vma=False,
    )
```

```python
import functools

import jax
import jax.numpy as jnp
from jax import lax
from jax.experimental import pallas as pl
from jax.experimental.pallas import tpu as pltpu
from jax.sharding import PartitionSpec as P

BOTH = ("section", "replica")
VMEM = pltpu.VMEM
SMEM = pltpu.SMEM


def spread(x, axis, root):
    mine = lax.axis_index(axis) == root
    return lax.psum(jnp.where(mine, x, jnp.zeros_like(x)), axis)


def add_tiles(summed, received, adj_tiles, row_ids, col_ids, first_slot, count, levels):
    tile_part = lax.dynamic_slice_in_dim(adj_tiles, first_slot, count, 0)
    row_pick = lax.dynamic_slice_in_dim(row_ids, first_slot, count, 0)
    col_pick = lax.dynamic_slice_in_dim(col_ids, first_slot, count, 0)
    picked = received[col_pick]
    products = jnp.einsum("kab,kbd->kad", tile_part, picked, preferred_element_type=jnp.float32)
    onehot = (row_pick[:, None] == levels[None, :]).astype(jnp.float32)
    return summed + jnp.einsum("kr,kad->rad", onehot, products, precision=lax.Precision.HIGHEST)


def general_shards(features, adj_tiles, tile_index, weight, bias_vec, grad_out):
    replicas = lax.axis_size("replica")
    replica_idx = lax.axis_index("replica")
    own_slab = lax.all_gather(features, "replica", axis=0, tiled=True)
    rows_slab, feat_width = own_slab.shape
    block_size = adj_tiles.shape[1]
    row_blocks = rows_slab // block_size
    turn_count = lax.axis_size("section") // replicas
    slot_count = adj_tiles.shape[0] // turn_count
    row_ids = tile_index[:, 0]
    col_ids = tile_index[:, 1]
    levels = jnp.arange(row_blocks, dtype=jnp.int32)

    def turn_step(step_idx, summed):
        received = spread(own_slab, "section", replica_idx * turn_count + step_idx)
        received = received.reshape(row_blocks, block_size, feat_width)
        first_slot = step_idx * slot_count
        return add_tiles(
            summed, received, adj_tiles, row_ids, col_ids, first_slot, slot_count, levels
        )

    start_sum = jnp.zeros((row_blocks, block_size, feat_width), jnp.float32)
    partial_sum = lax.fori_loop(0, turn_count, turn_step, start_sum).reshape(rows_slab, feat_width)
    share = rows_slab // replicas
    whole_sum = lax.psum(partial_sum, "replica")
    local_rows = lax.dynamic_slice_in_dim(whole_sum, replica_idx * share, share, 0)
    hidden = local_rows.astype(jnp.bfloat16)
    pre_act = jnp.dot(hidden, weight, preferred_element_type=jnp.float32) + bias_vec
    output = jax.nn.silu(pre_act).astype(jnp.bfloat16)
    sigma = jax.nn.sigmoid(pre_act)
    grad_pre = grad_out.astype(jnp.float32) * sigma * (1.0 + pre_act * (1.0 - sigma))
    grad_low = grad_pre.astype(jnp.bfloat16)
    weight_term = jnp.einsum("nd,ne->de", hidden, grad_low, preferred_element_type=jnp.float32)
    grad_weight, grad_bias = lax.psum((weight_term, jnp.sum(grad_pre, axis=0)), BOTH)
    return (output, grad_weight, grad_bias)


def send(x, target, name):
    perm = [(2 * p + c, 2 * target(p, c) + c) for p in range(16) for c in range(2)]
    with jax.named_scope(name):
        return lax.ppermute(x, BOTH, perm)


def swap(x, name):
    with jax.named_scope(name):
        return lax.ppermute(x, "replica", [(0, 1), (1, 0)])


def first_hop(x, name):
    return send(x, lambda p, c: p ^ (1 if c == 0 else 2), name)


def second_hop(x, name):
    return send(x, lambda p, c: p ^ (2 if c == 0 else 1), name)


def diagonal(x, name):
    return send(x, lambda p, c: p ^ 3, name)


def along_z(x, k, name):
    return send(x, lambda p, c: p ^ (4 * k), name)


def join(own, near):
    return jnp.concatenate([own, near], axis=0)


def after(*arrays):
    return lax.optimization_barrier(arrays)


def narrow(x):
    return x.astype(jnp.bfloat16)


def rounded(x):
    return lax.reduce_precision(x, 8, 7)


def widen(x):
    return x.astype(jnp.float32)


def work_list(index, slots, row_blocks):
    chip = lax.axis_index("section")
    core = lax.axis_index("replica")
    half = row_blocks // 2
    count = index.shape[0] // 2
    tile = jnp.arange(2 * count, dtype=jnp.int32)
    source = tile // slots
    row, col = index[:, 0], index[:, 1]
    live = (row >= 0) & (col // half == core)
    apart = source ^ chip
    x_apart, y_apart, z_apart = apart & 1, (apart >> 1) & 1, apart >> 2
    near = jnp.where(core == 0, x_apart, y_apart)
    far = jnp.where(core == 0, y_apart, x_apart)
    groups = 9
    array = 2 * z_apart + far
    last = (array == 7) & (near == 1)
    group = jnp.where(live, array + last.astype(jnp.int32), groups)
    block = jnp.where(last, 0, half * near) + col % half
    mine = tile // count == core
    entry = (tile % count + jnp.where(mine, 0, count)) | (block << 8) | ((row ^ (half * core)) << 12)
    spare = row_blocks << 12
    sizes = jnp.sum((group[:, None] == jnp.arange(groups)[None, :]).astype(jnp.int32), axis=0)
    padded = (sizes + 1) // 2 * 2
    edge = jnp.arange(groups + 1)
    starts = jnp.sum(jnp.where(edge[None, :groups] < edge[:, None], padded[None, :], 0), axis=1)
    same = (group[:, None] == group[None, :]) & (tile[None, :] < tile[:, None])
    rank = jnp.sum(same.astype(jnp.int32), axis=1)
    base = jnp.sum(jnp.where(group[:, None] == edge[None, :groups], starts[None, :groups], 0), axis=1)
    place = jnp.where(live, base + rank, -1)
    length = 2 * count + 2 * groups
    hit = place[None, :] == jnp.arange(length, dtype=jnp.int32)[:, None]
    entries = spare + jnp.sum(jnp.where(hit, (entry - spare)[None, :], 0), axis=1)
    return entries, starts


def gather_kernel(count, entries, starts, own, other, out, sem):
    pairs = starts[9] // 2

    def fetch(m):
        tile = entries[m] & 255

        @pl.when(tile < count)
        def _():
            pltpu.make_async_copy(own.at[tile], out.at[m], sem).start()

        @pl.when(tile >= count)
        def _():
            pltpu.make_async_copy(other.at[tile - count], out.at[m], sem).start()

    def begin(j, carry):
        fetch(2 * j)
        fetch(2 * j + 1)
        return carry

    def finish(size):
        def step(j, carry):
            block = out.at[pl.ds(0, size)]
            pltpu.make_async_copy(own.at[pl.ds(0, size)], block, sem).wait()
            return carry

        return step

    lax.fori_loop(0, pairs, begin, 0)
    lax.fori_loop(0, pairs // 8, finish(16), 0)
    lax.fori_loop(0, pairs % 8, finish(2), 0)


def gather_tiles(entries, starts, own, other):
    size = own.shape[1]
    return pl.pallas_call(
        functools.partial(gather_kernel, own.shape[0]),
        out_shape=VMEM((entries.shape[0], size, size), own.dtype),
        in_specs=[pl.BlockSpec(memory_space=SMEM)] * 2 + [pl.BlockSpec(memory_space=pltpu.HBM)] * 2,
        out_specs=pl.BlockSpec(memory_space=VMEM),
        scratch_shapes=[pltpu.SemaphoreType.DMA],
        name="gather_tiles",
        compiler_params=pltpu.CompilerParams(vmem_limit_bytes=47 << 20),
        cost_estimate=pl.CostEstimate(flops=0, bytes_accessed=1 << 10, transcendentals=0),
    )(entries, starts, own, other)


def add_group(entries, lo, hi, tiles, blocks, acc):
    def product(m):
        at = pl.multiple_of(((entries[m] >> 8) & 15) * 128, 128)
        return jnp.dot(tiles[m], blocks[pl.ds(at, 128), :], preferred_element_type=jnp.float32)

    def add(first, count):
        products = [product(first + i) for i in range(count)]
        for i, p in enumerate(products):
            acc[entries[first + i] >> 12] += p

    def four(j, carry):
        add(lo + 4 * j, 4)
        return carry

    fours = (hi - lo) // 4
    lax.fori_loop(0, fours, four, 0)

    @pl.when((hi - lo) % 4 != 0)
    def _():
        add(lo + 4 * fours, 2)


def add_kernel(groups, fresh, entries, starts, tiles, *refs):
    arrays, acc = refs[: len(groups)], refs[-1]
    if fresh:
        acc[...] = jnp.zeros_like(acc)
    for g, array in zip(groups, arrays):
        add_group(entries, starts[g], starts[g + 1], tiles, array, acc)


def late_kernel(groups, entries, starts, tiles, *refs):
    arrays, (acc, give) = refs[: len(groups)], refs[len(groups) + 1 :]
    for g, array in zip(groups, arrays):
        add_group(entries, starts[g], starts[g + 1], tiles, array, acc)
    half = give.shape[0]
    give[...] = acc[half : 2 * half]


def whole(space):
    return pl.BlockSpec(memory_space=space)


def add_groups(work, arrays, groups, acc, row_blocks, name):
    entries, starts, tiles = work
    shape = VMEM((row_blocks + 1, 128, arrays[0].shape[1]), jnp.float32)
    fresh = acc is None
    return pl.pallas_call(
        functools.partial(add_kernel, groups, fresh),
        out_shape=shape,
        in_specs=[whole(SMEM)] * 2 + [whole(VMEM)] * (1 + len(arrays) + (not fresh)),
        out_specs=whole(VMEM),
        name=name,
        input_output_aliases={} if fresh else {3 + len(arrays): 0},
        compiler_params=pltpu.CompilerParams(vmem_limit_bytes=4 << 20),
        cost_estimate=pl.CostEstimate(flops=16 << 28, bytes_accessed=4 << 20, transcendentals=0),
    )(entries, starts, tiles, *arrays, *([] if fresh else [acc]))


def add_late(work, arrays, groups, acc, row_blocks):
    entries, starts, tiles = work
    half = VMEM((row_blocks // 2, 128, arrays[0].shape[1]), jnp.float32)
    return pl.pallas_call(
        functools.partial(late_kernel, groups),
        out_shape=(VMEM(acc.shape, jnp.float32), half),
        in_specs=[whole(SMEM)] * 2 + [whole(VMEM)] * (2 + len(arrays)),
        out_specs=(whole(VMEM),) * 2,
        name="add_late",
        input_output_aliases={3 + len(arrays): 0},
        compiler_params=pltpu.CompilerParams(vmem_limit_bytes=4 << 20),
        cost_estimate=pl.CostEstimate(flops=1 << 25, bytes_accessed=2 << 20, transcendentals=0),
    )(entries, starts, tiles, *arrays, acc)


def dense_kernel(core, mine, theirs, weight, bias, grad_out, output, keep, give, full):
    hidden = (mine[: theirs.shape[0]] + theirs[...]).reshape(grad_out.shape).astype(jnp.bfloat16)
    pre_act = jnp.dot(hidden, weight[...], preferred_element_type=jnp.float32) + bias[...]
    sigma = 1.0 / (1.0 + jnp.exp(-pre_act))
    output[...] = (pre_act * sigma).astype(jnp.bfloat16)
    grad_pre = grad_out[...].astype(jnp.float32) * sigma * (1.0 + pre_act * (1.0 - sigma))
    grad_low = grad_pre.astype(jnp.bfloat16)
    full[...] = lax.dot_general(
        hidden, grad_low, (((0,), (0,)), ((), ())), preferred_element_type=jnp.float32
    )
    sums = jnp.sum(grad_pre, axis=0, keepdims=True)
    sums = jnp.broadcast_to(sums, (8, sums.shape[1]))
    share = full.shape[0] // 2
    at = core[0]
    keep[:share] = full[pl.ds(pl.multiple_of(at * share, share), share), :]
    give[:share] = full[pl.ds(pl.multiple_of((1 - at) * share, share), share), :]
    keep[share:] = sums
    give[share:] = sums


def dense(core, mine, theirs, weight, bias, grad_out):
    width = weight.shape[0]
    part = VMEM((width // 2 + 8, width), jnp.float32)
    return pl.pallas_call(
        dense_kernel,
        out_shape=(jax.ShapeDtypeStruct(grad_out.shape, jnp.bfloat16), part, part),
        in_specs=[whole(SMEM)] + [whole(VMEM)] * 5,
        out_specs=(whole(VMEM),) * 3,
        scratch_shapes=[VMEM((width, width), jnp.float32)],
        name="dense",
        compiler_params=pltpu.CompilerParams(vmem_limit_bytes=16 << 20),
        cost_estimate=pl.CostEstimate(
            flops=1 << 27, bytes_accessed=2 << 20, transcendentals=1 << 17
        ),
    )(core.reshape(1), mine, theirs, weight, bias.reshape(1, width), grad_out)


def finish_kernel(core, part, rest, weight, bias):
    share = part.shape[0] - 8
    at = core[0]
    weight[pl.ds(pl.multiple_of(at * share, share), share), :] = part[:share]
    weight[pl.ds(pl.multiple_of((1 - at) * share, share), share), :] = rest[:share]

    @pl.when(at == 0)
    def _():
        bias[...] = part[pl.ds(share, 1), :]

    @pl.when(at != 0)
    def _():
        bias[...] = rest[pl.ds(share, 1), :]


def finish(core, part, rest):
    rows, width = part.shape
    return pl.pallas_call(
        finish_kernel,
        out_shape=(
            jax.ShapeDtypeStruct((2 * (rows - 8), width), jnp.float32),
            jax.ShapeDtypeStruct((1, width), jnp.float32),
        ),
        in_specs=[whole(SMEM)] + [whole(VMEM)] * 2,
        out_specs=(whole(VMEM),) * 2,
        name="finish",
        compiler_params=pltpu.CompilerParams(vmem_limit_bytes=4 << 20),
    )(core.reshape(1), part, rest)


def shards(features, adj_tiles, tile_index, weight, bias_vec, grad_out):
    core = lax.axis_index("replica")
    row_blocks = 2 * features.shape[0] // adj_tiles.shape[1]
    slots = adj_tiles.shape[0] // 8

    z1 = along_z(features, 1, "z1")
    z2 = along_z(features, 2, "z2")
    r0 = first_hop(features, "r0")
    r0, index = after(r0, tile_index)
    index = lax.all_gather(index, "replica", axis=0, tiled=True)
    pair0 = join(features, r0)
    q0 = second_hop(pair0, "q0")
    other_tiles = swap(adj_tiles, "tiles")
    pair0, again = after(pair0, features)
    z3 = along_z(again, 3, "z3")
    z1, index = after(z1, index)
    pair1 = join(z1, first_hop(z1, "r1"))
    q1 = along_z(q0, 1, "q1")
    z2, other_tiles = after(z2, other_tiles)
    r2 = first_hop(z2, "r2")
    q2a = second_hop(z2, "q2a")
    pair2 = join(z2, r2)
    q2a, other_tiles = after(q2a, other_tiles)
    q2 = join(q2a, second_hop(r2, "q2b"))
    z3, pair1, pair2, q0 = after(z3, pair1, pair2, q0)
    r3 = first_hop(z3, "r3")
    q3a = second_hop(z3, "q3a")
    pair3 = join(z3, r3)
    q1, pair3 = after(q1, pair3)
    q3b = second_hop(r3, "q3b")
    entries, starts = work_list(index, slots, row_blocks)
    tiles = gather_tiles(entries, starts, adj_tiles, other_tiles)
    work = (entries, starts, tiles)
    acc = add_groups(work, (pair0, q0, pair1), (0, 1, 2), None, row_blocks, "add_a")
    acc = add_groups(work, (q1, pair2), (3, 4), acc, row_blocks, "add_b")
    acc = add_groups(work, (q2, pair3, q3a), (5, 6, 7), acc, row_blocks, "add_c")
    mine, give = add_late(work, (q3b,), (8,), acc, row_blocks)
    theirs = swap(give, "rows")
    output, keep, give = dense(core, mine, theirs, weight, bias_vec, grad_out)
    part = keep + swap(give, "halves")
    low = narrow(part)
    near = widen(first_hop(low, "sum1"))
    far = widen(second_hop(low, "sum2"))
    across = widen(diagonal(low, "sumd"))
    part = (rounded(part) + across) + (near + far)
    low_part = part.astype(jnp.bfloat16)
    z_parts = [lax.reduce_precision(part, 8, 7)]
    z_parts += [along_z(low_part, k, f"sum{2 + k}").astype(jnp.float32) for k in (3, 2, 1)]
    part = (z_parts[0] + z_parts[3]) + (z_parts[2] + z_parts[1])
    rest = swap(part, "back")
    grad_weight, grad_bias = finish(core, part, rest)
    return output, grad_weight, grad_bias.reshape(bias_vec.shape)


def solution(mesh):
    placed = (
        P(BOTH, None),
        P(BOTH, None, None),
        P(BOTH, None),
        P(),
        P(),
        P(BOTH, None),
    )
    small = mesh.shape["section"] == 16 and mesh.shape["replica"] == 2
    return jax.shard_map(
        shards if small else general_shards,
        mesh=mesh,
        in_specs=placed,
        out_specs=(P(BOTH, None), P(), P()),
        check_vma=False,
    )
```
